32 devices in a mesh: row: 4 (over y, x), col: 8 (over z, core).
Axes of the slice: x: 2, y: 2, z: 4, core: 2. Of those that a mesh axis runs over, the one named last changes fastest.
Arguments:
- scalar_field: float32 [256, 256, 1024], P('col', 'row'), may hold values from -1.2 to 1.2
- reaction: float32 [256, 256, 1024], P('col', 'row'), may hold values from 0.5 to 4
- x_faces: float32 [1024], replicated, may hold values from 0.5 to 4
- y_faces: float32 [256], replicated, may hold values from 0.5 to 4
- z_faces: float32 [256], replicated, may hold values from 0.5 to 4
- x_inverse: float32 [8, 128, 128], replicated, may hold values from 0 to 1, as said below
- y_inverse: float32 [2, 128, 128], replicated, may hold values from 0 to 1, as said below
- z_inverse: float32 [2, 128, 128], replicated, may hold values from 0 to 1, as said below
Outputs:
- advanced: float32 [256, 256, 1024], P('col', 'row')
The draws below stay inside these ranges and needn't reach their ends.
Inputs may be any that keep to these rules, and one draw needn't show every extreme that they name: x_inverse[c] is, up to float32 rounding, the inverse of the block of rows and columns c * 128 to (c + 1) * 128 - 1 of the matrix I - 500 A_x along one x line. y_inverse[c] is, up to float32 rounding, the inverse of the block of rows and columns c * 128 to (c + 1) * 128 - 1 of the matrix I - 500 A_y along one y line. z_inverse[c] is, up to float32 rounding, the inverse of the block of rows and columns c * 128 to (c + 1) * 128 - 1 of the matrix I - 500 A_z along one z line.
All inputs are finite; a program needn't handle non-finite values.
Results may differ from the reference program's by a relative error of at most 0.0003.
Values sent between devices are 32-bit elements; how exact they have to be, the bound alone decides.
A program may use at most 128 MiB of HBM per device.

```python
import math
import jax
import jax.numpy as jnp
from jax import lax

NY = 256
NZ = 256
GROUP = 128
NX = 1024


implicit_weight = 0.5


time_step = 1000.0


def invert_small_drawn(matrix):
    order = matrix.shape[0]
    joined = jnp.concatenate([matrix, jnp.eye(order, dtype=matrix.dtype)], axis=1)

    def sweep(step_index, current):
        pivot_row = lax.dynamic_index_in_dim(current, step_index, 0, keepdims=False)
        pivot_row = pivot_row / lax.dynamic_index_in_dim(pivot_row, step_index, 0, keepdims=False)
        pivot_column = lax.dynamic_slice_in_dim(current, step_index, 1, 1)
        current = current - pivot_column * pivot_row[None, :]
        return lax.dynamic_update_index_in_dim(current, pivot_row, step_index, 0)
    joined = lax.fori_loop(0, order, sweep, joined)
    return joined[:, order:]


def faces_and_blocks(key, length):
    face_values = jnp.exp(jax.random.uniform(key, (length,), jnp.float32, math.log(0.5), math.log(4.0)))
    couple = implicit_weight * time_step * face_values
    couple_above = jnp.concatenate([couple[1:], jnp.zeros((1,), jnp.float32)])
    groups = length // GROUP
    diagonal = (1.0 + couple + couple_above).reshape(groups, GROUP)
    upper_band = couple_above.reshape(groups, GROUP)[:, :, None] * jnp.eye(GROUP, k=1, dtype=jnp.float32)
    blocks = diagonal[:, :, None] * jnp.eye(GROUP, dtype=jnp.float32) - upper_band - jnp.swapaxes(upper_band, 1, 2)
    return (face_values, jax.vmap(invert_small_drawn)(blocks))


def draw_x_faces(key, part):
    return faces_and_blocks(jax.random.fold_in(key, 101), NX)[0]


def draw_x_inverse(key, part):
    return faces_and_blocks(jax.random.fold_in(key, 101), NX)[1]


def draw_y_faces(key, part):
    return faces_and_blocks(jax.random.fold_in(key, 202), NY)[0]


def draw_y_inverse(key, part):
    return faces_and_blocks(jax.random.fold_in(key, 202), NY)[1]


def draw_z_faces(key, part):
    return faces_and_blocks(jax.random.fold_in(key, 303), NZ)[0]


def draw_z_inverse(key, part):
    return faces_and_blocks(jax.random.fold_in(key, 303), NZ)[1]


def levels(stream_key, dims, cuts, least, high):
    def one(position, parts):
        heights = jax.random.uniform(jax.random.fold_in(jax.random.fold_in(stream_key, 6), position), (parts,), jnp.float32, least / len(cuts), high / len(cuts))
        return jnp.repeat(jnp.exp(heights), dims[position] // parts).reshape((-1,) + (1,) * (len(dims) - position - 1))

    level = one(*cuts[0])
    for cut in cuts[1:]:
        level = level * one(*cut)
    return level


def setup_inputs(seed: int = 0) -> dict:
    seeds = jax.random.split(jax.random.key(seed), 9)
    return {
        "scalar_field": jnp.clip(jax.random.uniform(seeds[0], (NZ, NY, NX), jnp.float32, -1.2, 1.2) * levels(seeds[0], (NZ, NY, NX), ((0, 8), (1, 4)), -0.4, 0.0), -1.2, 1.2),
        "reaction": jnp.clip(jnp.exp(math.log(4.0) - 2.0794415 * jax.random.uniform(seeds[1], (NZ, NY, NX), jnp.float32) ** levels(seeds[1], (NZ, NY, NX), ((0, 8), (1, 4)), -0.2, 0.2)), 0.5, 4.0),
        "x_faces": draw_x_faces(jax.random.fold_in(seeds[8], 71), 0),
        "y_faces": draw_y_faces(jax.random.fold_in(seeds[8], 71), 0),
        "z_faces": draw_z_faces(jax.random.fold_in(seeds[8], 71), 0),
        "x_inverse": draw_x_inverse(jax.random.fold_in(seeds[8], 71), 0),
        "y_inverse": draw_y_inverse(jax.random.fold_in(seeds[8], 71), 0),
        "z_inverse": draw_z_inverse(jax.random.fold_in(seeds[8], 71), 0),
    }


implicit_weight = 0.5
time_step = 1000.0


def shift_lower(values, line_axis):
    length = values.shape[line_axis]
    first_slot = jnp.zeros_like(lax.slice_in_dim(values, 0, 1, axis=line_axis))
    return jnp.concatenate([first_slot, lax.slice_in_dim(values, 0, length - 1, axis=line_axis)], axis=line_axis)


def shift_upper(values, line_axis):
    length = values.shape[line_axis]
    last_slot = jnp.zeros_like(lax.slice_in_dim(values, 0, 1, axis=line_axis))
    return jnp.concatenate([lax.slice_in_dim(values, 1, length, axis=line_axis), last_slot], axis=line_axis)


def apply_line(values, face_values, line_axis):
    spread = [1, 1, 1]
    spread[line_axis] = values.shape[line_axis]
    face_here = face_values.reshape(spread)
    face_next = jnp.concatenate([face_values[1:], jnp.zeros((1,), face_values.dtype)]).reshape(spread)
    lower_value = shift_lower(values, line_axis)
    upper_value = shift_upper(values, line_axis)
    return face_next * (upper_value - values) - face_here * (values - lower_value)


def invert_small(matrix):
    order = matrix.shape[0]
    joined = jnp.concatenate([matrix, jnp.eye(order, dtype=matrix.dtype)], axis=1)

    def sweep(step_index, current):
        pivot_row = lax.dynamic_index_in_dim(current, step_index, 0, keepdims=False)
        pivot_row = pivot_row / lax.dynamic_index_in_dim(pivot_row, step_index, 0, keepdims=False)
        pivot_column = lax.dynamic_slice_in_dim(current, step_index, 1, 1)
        current = current - pivot_column * pivot_row[None, :]
        return lax.dynamic_update_index_in_dim(current, pivot_row, step_index, 0)

    joined = lax.fori_loop(0, order, sweep, joined)
    return joined[:, order:]


def reduced_inverse(inverse, coupling_before, coupling_after):
    groups, block_width = inverse.shape[0], inverse.shape[1]
    order = 2 * groups
    group_index = jnp.arange(groups)
    lead_rows = 2 * group_index
    trail_rows = 2 * group_index + 1
    prev_cols = jnp.maximum(2 * group_index - 1, 0)
    next_cols = jnp.minimum(2 * group_index + 2, order - 1)
    coupled = jnp.zeros((order, order), inverse.dtype)
    coupled = coupled.at[lead_rows, prev_cols].add(coupling_before * inverse[:, 0, 0])
    coupled = coupled.at[lead_rows, next_cols].add(coupling_after * inverse[:, 0, block_width - 1])
    coupled = coupled.at[trail_rows, prev_cols].add(coupling_before * inverse[:, block_width - 1, 0])
    coupled = coupled.at[trail_rows, next_cols].add(coupling_after * inverse[:, block_width - 1, block_width - 1])
    return invert_small(jnp.eye(order, dtype=inverse.dtype) - coupled)


def line_solve(right_side, inverse, face_values, line_axis):
    groups, block_width = inverse.shape[0], inverse.shape[1]
    dims_full = right_side.shape
    blocked = right_side.reshape(dims_full[:line_axis] + (groups, block_width) + dims_full[line_axis + 1:])
    others = ["u", "v"]
    source = "".join(others[:line_axis] + ["c", "j"] + others[line_axis:])
    target = "".join(others[:line_axis] + ["c", "i"] + others[line_axis:])
    inside = jnp.einsum("cij," + source + "->" + target, inverse, blocked, precision=lax.Precision.HIGHEST)
    leading = lax.index_in_dim(inside, 0, line_axis + 1, keepdims=False)
    trailing = lax.index_in_dim(inside, block_width - 1, line_axis + 1, keepdims=False)
    coupling = implicit_weight * time_step * face_values[block_width::block_width]
    nothing = jnp.zeros((1,), face_values.dtype)
    coupling_before = jnp.concatenate([nothing, coupling])
    coupling_after = jnp.concatenate([coupling, nothing])
    reduced = reduced_inverse(inverse, coupling_before, coupling_after)
    interface = jnp.stack([leading, trailing], axis=line_axis + 1)
    interface = interface.reshape(dims_full[:line_axis] + (2 * groups,) + dims_full[line_axis + 1:])
    end_source = "".join(others[:line_axis] + ["j"] + others[line_axis:])
    end_target = "".join(others[:line_axis] + ["i"] + others[line_axis:])
    solved = jnp.einsum("ij," + end_source + "->" + end_target, reduced, interface, precision=lax.Precision.HIGHEST)
    solved = solved.reshape(dims_full[:line_axis] + (groups, 2) + dims_full[line_axis + 1:])
    first_values = lax.index_in_dim(solved, 0, line_axis + 1, keepdims=False)
    last_values = lax.index_in_dim(solved, 1, line_axis + 1, keepdims=False)
    prev_last = shift_lower(last_values, line_axis)
    next_first = shift_upper(first_values, line_axis)
    spike_shape = [1, 1, 1, 1]
    spike_shape[line_axis] = groups
    spike_shape[line_axis + 1] = block_width
    left_spike = (coupling_before[:, None] * inverse[:, :, 0]).reshape(spike_shape)
    right_spike = (coupling_after[:, None] * inverse[:, :, block_width - 1]).reshape(spike_shape)
    result = inside + left_spike * jnp.expand_dims(prev_last, line_axis + 1) + right_spike * jnp.expand_dims(next_first, line_axis + 1)
    return result.reshape(dims_full)


def reference(scalar_field, reaction, x_faces, y_faces, z_faces, x_inverse, y_inverse, z_inverse):
    x_term = apply_line(scalar_field, x_faces, 2)
    y_term = apply_line(scalar_field, y_faces, 1)
    z_term = apply_line(scalar_field, z_faces, 0)
    source = reaction * scalar_field * (1.0 - scalar_field * scalar_field)
    explicit = scalar_field + time_step * (x_term + y_term + z_term + source) - implicit_weight * time_step * x_term
    first_section = line_solve(explicit, x_inverse, x_faces, 2)
    second_section = line_solve(first_section - implicit_weight * time_step * y_term, y_inverse, y_faces, 1)
    return line_solve(second_section - implicit_weight * time_step * z_term, z_inverse, z_faces, 0)
```

```python
import functools

import jax
import jax.numpy as jnp
from jax import lax
from jax.experimental import pallas as pl
from jax.experimental.pallas import tpu as pltpu
from jax.sharding import PartitionSpec as P

WEIGHT = 0.5
STEP = 1000.0
MESH = pl.DeviceIdType.MESH
VMEM_LIMIT = 60 * 1024 * 1024


def shifted(a, by, fill):
    n = a.shape[1]
    lane = lax.broadcasted_iota(jnp.int32, a.shape, 1)
    if by > 0:
        return jnp.where(lane >= by, pltpu.roll(a, by, 1), fill)
    return jnp.where(lane < n + by, pltpu.roll(a, n + by, 1), fill)


def running_sum(a):
    by = 1
    while by < a.shape[1]:
        a = a + shifted(a, by, 0.0)
        by *= 2
    return a


def ladder(couple, sign):
    p00, p01, p10, p11 = 1.0 + couple, couple, jnp.ones_like(couple), couple
    by = 1
    while by < couple.shape[1]:
        q00, q01 = shifted(p00, sign * by, 1.0), shifted(p01, sign * by, 0.0)
        q10, q11 = shifted(p10, sign * by, 0.0), shifted(p11, sign * by, 1.0)
        n00, n01 = p00 * q00 + p01 * q10, p00 * q01 + p01 * q11
        n10, n11 = p10 * q00 + p11 * q10, p10 * q01 + p11 * q11
        scale = 1.0 / (n00 + n01 + n10 + n11)
        p00, p01, p10, p11 = n00 * scale, n01 * scale, n10 * scale, n11 * scale
        by *= 2
    return p00 / p10


def ladder_kernel(faces_ref, out_ref):
    here = WEIGHT * STEP * faces_ref[...]
    above = shifted(here, -1, 0.0)
    e = ladder(here, 1)
    h = ladder(above, -1)
    pivot = above + e
    up = here / (here + h)
    down = above / pivot
    out_ref[0:8] = 1.0 / (e + h - 1.0)
    out_ref[8:16] = running_sum(jnp.log(jnp.maximum(up, 1e-30)))
    out_ref[16:24] = running_sum(jnp.log(jnp.maximum(down, 1e-30)))
    out_ref[24:32] = 1.0 / pivot
    out_ref[32:40] = down


def split(a):
    high = a.astype(jnp.bfloat16)
    return high, (a - high.astype(jnp.float32)).astype(jnp.bfloat16)


def dot(a, b):
    return jnp.dot(a, b, preferred_element_type=jnp.float32)


def sweep_kernel(
    planes, zco_ref, kz_ref, u_ref, before_ref, after_ref, zlo_ref, zhi_ref, ylo_ref, yhi_ref,
    rea_ref, kx_ref, ky_ref, xh_ref, xl_ref, xp_ref, ym_ref, v_ref, ye_ref, ze_ref,
):
    step, steps = pl.program_id(0), pl.num_programs(0)
    _, yc, nx = u_ref.shape
    zc = v_ref.shape[0]
    nb, bx = xh_ref.shape[0], xh_ref.shape[1]
    kx, kxn = kx_ref[0:1], kx_ref[1:2]
    ky, kyn = ky_ref[:, 0:1], ky_ref[:, 1:2]
    lane = lax.broadcasted_iota(jnp.int32, (yc, nx), 1)
    sub = lax.broadcasted_iota(jnp.int32, (yc, nx), 0)

    @pl.when(step == 0)
    def _():
        v_ref[0] = jnp.zeros((yc, nx), jnp.float32)

    below = jnp.where(step == 0, zlo_ref[0], before_ref[0])
    above_last = jnp.where(step == steps - 1, zhi_ref[0], after_ref[0])
    changes = []
    for p in range(planes):
        z = step * planes + p
        u = u_ref[p]
        above = u_ref[p + 1] if p + 1 < planes else above_last
        left = jnp.where(lane == 0, 0.0, pltpu.roll(u, 1, 1))
        right = pltpu.roll(u, nx - 1, 1)
        down = jnp.where(sub == 0, ylo_ref[p], pltpu.roll(u, 1, 0))
        upper = jnp.where(sub == yc - 1, yhi_ref[p], pltpu.roll(u, yc - 1, 0))
        total = kxn * (right - u) - kx * (u - left)
        total += kyn * (upper - u) - ky * (u - down)
        total += kz_ref[1, z] * (above - u) - kz_ref[0, z] * (u - below)
        total += rea_ref[p] * u * (1.0 - u * u)
        changes.append(STEP * total)
        below = u
    change = jnp.concatenate(changes, axis=0) if planes > 1 else changes[0]
    local = []
    for b in range(nb):
        high, low = split(change[:, b * bx:(b + 1) * bx])
        local.append(dot(high, xh_ref[b]) + (dot(high, xl_ref[b]) + dot(low, xh_ref[b])))
    rows = planes * yc
    from_left = [jnp.zeros((rows, 1), jnp.float32)]
    from_right = [jnp.zeros((rows, 1), jnp.float32)]
    for b in range(nb - 1):
        through = xp_ref[0:1, (b + 1) * bx - 1:(b + 1) * bx]
        from_left.append(from_left[-1] * through + local[b][:, bx - 1:bx])
        c = nb - 1 - b
        through = xp_ref[1:2, c * bx:c * bx + 1]
        from_right.append(from_right[-1] * through + local[c][:, 0:1])
    from_right.reverse()
    solved = jnp.concatenate(
        [
            local[b]
            + xp_ref[0:1, b * bx:(b + 1) * bx] * from_left[b]
            + xp_ref[1:2, b * bx:(b + 1) * bx] * from_right[b]
            for b in range(nb)
        ],
        axis=1,
    )
    carry = v_ref[jnp.maximum(step * planes - 1, 0)]
    for p in range(planes):
        z = step * planes + p
        high, low = split(solved[p * yc:(p + 1) * yc])
        w = dot(ym_ref[...], jnp.concatenate([high, low, high], axis=0))
        carry = zco_ref[0, z] * w + zco_ref[1, z] * carry
        v_ref[z] = carry

    @pl.when(step == steps - 1)
    def _():
        wide = 256 if nx % 256 == 0 else nx
        for x in range(nx // wide):
            cols = slice(x * wide, (x + 1) * wide)
            top = v_ref[zc - 1, :, cols]
            ze_ref[1, :, cols] = top
            ye_ref[0, zc - 1:zc, cols] = top[0:1]
            ye_ref[1, zc - 1:zc, cols] = top[yc - 1:yc]

            def back(i, value):
                z = zc - 2 - i
                value = v_ref[z, :, cols] + zco_ref[2, z] * value
                v_ref[z, :, cols] = value
                ye_ref[0, pl.ds(z, 1), cols] = value[0:1]
                ye_ref[1, pl.ds(z, 1), cols] = value[yc - 1:yc]
                return value

            ze_ref[0, :, cols] = lax.fori_loop(0, zc - 1, back, top)


def exchange_kernel(
    nr, nc, chunks, yw_ref, zw_ref, yp_ref, ye_ref, ze_ref, sy_ref, sz_ref,
    ybuf, zbuf, zsend, ysend_sem, yrecv_sem, zsend_sem, zrecv_sem,
):
    row, col = lax.axis_index("row"), lax.axis_index("col")
    zc, nx = ye_ref.shape[1], ye_ref.shape[2]
    yc = ze_ref.shape[1]
    has_low, has_high = col > 0, col < nc - 1
    barrier = pltpu.get_barrier_semaphore()
    for other in range(nr):
        @pl.when(other != row)
        def _():
            pl.semaphore_signal(barrier, inc=1, device_id=(other, col), device_id_type=MESH)

    @pl.when(has_low)
    def _():
        pl.semaphore_signal(barrier, inc=1, device_id=(row, col - 1), device_id_type=MESH)

    @pl.when(has_high)
    def _():
        pl.semaphore_signal(barrier, inc=1, device_id=(row, col + 1), device_id_type=MESH)

    pl.semaphore_wait(barrier, nr - 1 + has_low.astype(jnp.int32) + has_high.astype(jnp.int32))

    def y_copy(side, other, slot):
        return pltpu.make_async_remote_copy(
            src_ref=ye_ref.at[1 - side],
            dst_ref=ybuf.at[side, slot],
            send_sem=ysend_sem.at[side, other],
            recv_sem=yrecv_sem.at[side, slot],
            device_id=(other, col),
            device_id_type=MESH,
        )

    for other in range(nr):
        @pl.when(other > row)
        def _():
            y_copy(0, other, row).start()

        @pl.when(other < row)
        def _():
            y_copy(1, other, row).start()

    sy_ref[...] = jnp.zeros_like(sy_ref)
    for other in range(nr):
        @pl.when(other < row)
        def _():
            y_copy(0, other, other).wait_recv()
            sy_ref[0] += yw_ref[0, other] * ybuf[0, other]

        @pl.when(other > row)
        def _():
            y_copy(1, other, other).wait_recv()
            sy_ref[1] += yw_ref[1, other] * ybuf[1, other]

    yb, ya = yp_ref[:, 0:1], yp_ref[:, 1:2]
    part = yc // chunks

    def z_copy(side, k):
        rows = pl.ds(k * part, part)
        return pltpu.make_async_remote_copy(
            src_ref=zsend.at[side, rows],
            dst_ref=zbuf.at[side, rows],
            send_sem=zsend_sem.at[side, k],
            recv_sem=zrecv_sem.at[side, k],
            device_id=(row, col + (1 - 2 * side)),
            device_id_type=MESH,
        )

    def scan(side):
        source, target = (has_low, has_high) if side == 0 else (has_high, has_low)
        edge, z = (1, zc - 1) if side == 0 else (0, 0)
        for k in range(chunks):
            rows = slice(k * part, (k + 1) * part)

            @pl.when(source)
            def _():
                z_copy(side, k).wait_recv()
                sz_ref[side, rows] = zbuf[side, rows]

            @pl.when(jnp.logical_not(source))
            def _():
                sz_ref[side, rows] = jnp.zeros((part, nx), jnp.float32)

            @pl.when(target)
            def _():
                value = ze_ref[edge, rows] + yb[rows] * sy_ref[0, z:z + 1]
                value += ya[rows] * sy_ref[1, z:z + 1]
                zsend[side, rows] = value + zw_ref[side] * sz_ref[side, rows]
                z_copy(side, k).start()

    low_half = col < nc // 2

    @pl.when(low_half)
    def _():
        scan(0)

    scan(1)

    @pl.when(jnp.logical_not(low_half))
    def _():
        scan(0)

    for k in range(chunks):
        @pl.when(has_high)
        def _():
            z_copy(0, k).wait_send()

        @pl.when(has_low)
        def _():
            z_copy(1, k).wait_send()

    for other in range(nr):
        @pl.when(other > row)
        def _():
            y_copy(0, other, row).wait_send()

        @pl.when(other < row)
        def _():
            y_copy(1, other, row).wait_send()


def finish_kernel(planes, zp_ref, u_ref, v_ref, yp_ref, sy_ref, sz_ref, out_ref):
    yb, ya = yp_ref[:, 0:1], yp_ref[:, 1:2]
    for p in range(planes):
        z = pl.program_id(0) * planes + p
        value = u_ref[p] + v_ref[p]
        value += yb * sy_ref[0, pl.ds(z, 1)] + ya * sy_ref[1, pl.ds(z, 1)]
        out_ref[p] = value + zp_ref[0, z] * sz_ref[0] + zp_ref[1, z] * sz_ref[1]


def blocks_of_inverse(diagonal, sums):
    n = diagonal.shape[-1]
    i = lax.broadcasted_iota(jnp.int32, (n, n), 0)
    j = lax.broadcasted_iota(jnp.int32, (n, n), 1)
    near = jnp.where(i >= j, diagonal[..., None, :], diagonal[..., :, None])
    return near * jnp.exp(-jnp.abs(sums[..., :, None] - sums[..., None, :]))


def halves(a):
    high = lax.reduce_precision(a, 8, 7)
    return high.astype(jnp.bfloat16), (a - high).astype(jnp.bfloat16)


def body(u, reaction, x_faces, y_faces, z_faces, x_inverse, y_inverse, z_inverse):
    zc, yc, nx = u.shape
    nr, nc = lax.axis_size("row"), lax.axis_size("col")
    row, col = lax.axis_index("row"), lax.axis_index("col")
    ny, nz = y_faces.shape[0], z_faces.shape[0]
    f32 = jnp.float32

    def up(n):
        return [(i, i + 1) for i in range(n - 1)]

    def down(n):
        return [(i + 1, i) for i in range(n - 1)]

    ylo = lax.ppermute(u[:, yc - 1:yc], "row", up(nr))
    yhi = lax.ppermute(u[:, 0:1], "row", down(nr))
    zlo = lax.ppermute(u[zc - 1:zc], "col", up(nc))
    zhi = lax.ppermute(u[0:1], "col", down(nc))

    longest = -(-max(nx, ny, nz) // 128) * 128
    faces = jnp.stack([jnp.pad(f, (0, longest - f.shape[0])) for f in (x_faces, y_faces, z_faces)])
    faces = jnp.pad(faces, ((0, 5), (0, 0)))
    tables = pl.pallas_call(
        ladder_kernel, out_shape=jax.ShapeDtypeStruct((40, longest), f32)
    )(faces).reshape(5, 8, longest)

    bx = 256 if nx % 256 == 0 else nx
    nb = nx // bx
    diag, up_sum, down_sum = (tables[i, 0, :nx].reshape(nb, bx) for i in range(3))
    xh, xl = halves(blocks_of_inverse(diag, up_sum))
    zero = jnp.zeros((1,), f32)
    up_start = jnp.concatenate([zero, up_sum[:-1, -1]])[:, None]
    down_before = jnp.concatenate([zero, tables[2, 0, :nx - 1]]).reshape(nb, bx)
    xp = jnp.stack([jnp.exp(up_sum - up_start), jnp.exp(down_sum[:, -1:] - down_before)])
    xp = xp.reshape(2, nx)
    kx = jnp.stack([x_faces, jnp.concatenate([x_faces[1:], zero])])

    def own(values, start, count):
        return lax.dynamic_slice_in_dim(values, start, count)

    def passes(which, n, start, count):
        ups = jnp.concatenate([zero, tables[1, which, :n]])
        downs = jnp.concatenate([zero, tables[2, which, :n]])
        ups_here, downs_here = own(ups, start, count + 1), own(downs, start, count + 1)
        onward = jnp.exp(ups_here[1:] - ups_here[0])
        backward = jnp.exp(downs_here[count] - downs_here[:count])
        return ups, downs, ups_here, downs_here, onward, backward

    y0 = row * yc
    ups, downs, ups_here, downs_here, onward, backward = passes(1, ny, y0, yc)
    yh, yl = halves(blocks_of_inverse(own(tables[0, 1, :ny], y0, yc), ups_here[1:]))
    ym = jnp.concatenate([yh, yh, yl], axis=1)
    yp = jnp.stack([onward, backward], axis=1)
    who = jnp.arange(nr)
    from_low = jnp.where(who < row, jnp.exp(jnp.minimum(ups_here[0] - ups[yc::yc], 0.0)), 0.0)
    from_high = jnp.where(who > row, jnp.exp(jnp.minimum(downs[:-1:yc] - downs_here[yc], 0.0)), 0.0)
    yw = jnp.stack([from_low, from_high])
    yf = jnp.concatenate([y_faces, zero])
    ky = jnp.stack([own(yf, y0, yc), own(yf, y0 + 1, yc)], axis=1)

    z0 = col * zc
    _, _, _, _, z_onward, z_backward = passes(2, nz, z0, zc)
    zp = jnp.stack([z_onward, z_backward])
    zw = jnp.stack([z_onward[-1], z_backward[0]])
    zf = jnp.concatenate([z_faces, zero])
    kz = jnp.stack([own(zf, z0, zc), own(zf, z0 + 1, zc)])
    at = jnp.arange(zc)
    over = jnp.where(at == zc - 1, own(tables[0, 2, :nz], z0, zc), own(tables[3, 2, :nz], z0, zc))
    into = jnp.where(at == 0, 0.0, WEIGHT * STEP * kz[0] * over)
    zco = jnp.stack([over, into, own(tables[4, 2, :nz], z0, zc)])

    planes = 2 if zc % 2 == 0 else 1
    steps = zc // planes
    smem = pl.BlockSpec(memory_space=pltpu.SMEM)
    vmem = pl.BlockSpec(memory_space=pltpu.VMEM)
    plane = (1, yc, nx)

    def whole(*shape):
        return pl.BlockSpec(shape, lambda s: (0,) * len(shape))

    slab = pl.BlockSpec((planes, yc, nx), lambda s: (s, 0, 0))
    line = pl.BlockSpec((planes, 1, nx), lambda s: (s, 0, 0))
    v, ye, ze = pl.pallas_call(
        functools.partial(sweep_kernel, planes),
        grid=(steps,),
        in_specs=[
            smem, smem, slab,
            pl.BlockSpec(plane, lambda s: (jnp.maximum(s * planes - 1, 0), 0, 0)),
            pl.BlockSpec(plane, lambda s: (jnp.minimum((s + 1) * planes, zc - 1), 0, 0)),
            whole(*plane), whole(*plane), line, line, slab,
            whole(2, nx), whole(yc, 2), whole(nb, bx, bx), whole(nb, bx, bx), whole(2, nx),
            whole(yc, 3 * yc),
        ],
        out_specs=[whole(zc, yc, nx), whole(2, zc, nx), whole(2, yc, nx)],
        out_shape=[
            jax.ShapeDtypeStruct((zc, yc, nx), f32),
            jax.ShapeDtypeStruct((2, zc, nx), f32),
            jax.ShapeDtypeStruct((2, yc, nx), f32),
        ],
        compiler_params=pltpu.CompilerParams(vmem_limit_bytes=VMEM_LIMIT),
    )(zco, kz, u, u, u, zlo, zhi, ylo, yhi, reaction, kx, ky, xh, xl, xp, ym)

    chunks = 4 if yc % 32 == 0 else 1
    sy, sz = pl.pallas_call(
        functools.partial(exchange_kernel, nr, nc, chunks),
        in_specs=[smem, smem, vmem, vmem, vmem],
        out_specs=[vmem, vmem],
        out_shape=[
            jax.ShapeDtypeStruct((2, zc, nx), f32),
            jax.ShapeDtypeStruct((2, yc, nx), f32),
        ],
        scratch_shapes=[
            pltpu.VMEM((2, nr, zc, nx), f32),
            pltpu.VMEM((2, yc, nx), f32),
            pltpu.VMEM((2, yc, nx), f32),
            pltpu.SemaphoreType.DMA((2, nr)),
            pltpu.SemaphoreType.DMA((2, nr)),
            pltpu.SemaphoreType.DMA((2, chunks)),
            pltpu.SemaphoreType.DMA((2, chunks)),
        ],
        compiler_params=pltpu.CompilerParams(
            collective_id=0, has_side_effects=True, vmem_limit_bytes=VMEM_LIMIT
        ),
    )(yw, zw, yp, ye, ze)

    return pl.pallas_call(
        functools.partial(finish_kernel, planes),
        grid=(steps,),
        in_specs=[smem, slab, slab, whole(yc, 2), whole(2, zc, nx), whole(2, yc, nx)],
        out_specs=slab,
        out_shape=jax.ShapeDtypeStruct((zc, yc, nx), f32),
        compiler_params=pltpu.CompilerParams(vmem_limit_bytes=VMEM_LIMIT),
    )(zp, u, v, yp, sy, sz)


def solution(mesh):
    in_specs = (P("col", "row", None), P("col", "row", None), P(), P(), P(), P(), P(), P())
    out_specs = P("col", "row", None)
    return jax.shard_map(body, mesh=mesh, in_specs=in_specs, out_specs=out_specs, check_vma=False)
```

```python
import functools

import jax
import jax.numpy as jnp
from jax import lax
from jax.experimental import pallas as pl
from jax.experimental.pallas import tpu as pltpu
from jax.sharding import PartitionSpec as P

WEIGHT = 0.5
STEP = 1000.0
MESH = pl.DeviceIdType.MESH
VMEM_LIMIT = 24 * 1024 * 1024


def shifted(a, by, fill):
    n = a.shape[1]
    lane = lax.broadcasted_iota(jnp.int32, a.shape, 1)
    if by > 0:
        return jnp.where(lane >= by, pltpu.roll(a, by, 1), fill)
    return jnp.where(lane < n + by, pltpu.roll(a, n + by, 1), fill)


def running_sum(a):
    by = 1
    while by < a.shape[1]:
        a = a + shifted(a, by, 0.0)
        by *= 2
    return a


def ladder(couple, sign):
    p00, p01, p10, p11 = 1.0 + couple, couple, jnp.ones_like(couple), couple
    by = 1
    while by < couple.shape[1]:
        q00, q01 = shifted(p00, sign * by, 1.0), shifted(p01, sign * by, 0.0)
        q10, q11 = shifted(p10, sign * by, 0.0), shifted(p11, sign * by, 1.0)
        n00, n01 = p00 * q00 + p01 * q10, p00 * q01 + p01 * q11
        n10, n11 = p10 * q00 + p11 * q10, p10 * q01 + p11 * q11
        scale = 1.0 / (n00 + n01 + n10 + n11)
        p00, p01, p10, p11 = n00 * scale, n01 * scale, n10 * scale, n11 * scale
        by *= 2
    return p00 / p10


def as_column(line, rows):
    n = line.shape[1]
    return jnp.transpose(jnp.broadcast_to(line, (n, n)))[:rows, :rows]


def block_of_inverse(diagonal, sums, n):
    i = lax.broadcasted_iota(jnp.int32, (n, n), 0)
    j = lax.broadcasted_iota(jnp.int32, (n, n), 1)
    near = jnp.where(i >= j, diagonal[:, :n], as_column(diagonal, n))
    return near * jnp.exp(-jnp.abs(as_column(sums, n) - sums[:, :n]))


def table_kernel(
    nr, zc, yc, pos_ref, faces_ref, field_ref, xh_ref, xl_ref, xp_ref, ym_ref, yt_ref, zt_ref,
    held_ref, sem,
):
    fetch = pltpu.make_async_copy(field_ref, held_ref, sem)
    fetch.start()
    row, col = pos_ref[0], pos_ref[1]
    faces = faces_ref[...]
    length = faces.shape[1]
    nb, bx = xh_ref.shape[0], xh_ref.shape[1]
    nx = nb * bx
    here = WEIGHT * STEP * faces
    above = shifted(here, -1, 0.0)
    e = ladder(here, 1)
    h = ladder(above, -1)
    pivot = above + e
    down = above / pivot
    inverse = 1.0 / pivot
    diag = 1.0 / (e + h - 1.0)
    ups = running_sum(jnp.log(jnp.maximum(here / (here + h), 1e-30)))
    downs = running_sum(jnp.log(jnp.maximum(down, 1e-30)))
    ups_before, downs_before = shifted(ups, 1, 0.0), shifted(downs, 1, 0.0)
    next_faces = shifted(faces, -1, 0.0)

    xp_ref[2:3] = faces[0:1, :nx]
    xp_ref[3:4] = next_faces[0:1, :nx]
    for b in range(nb):
        first, last = b * bx, (b + 1) * bx - 1
        cols = slice(first, last + 1)
        high, low = split(block_of_inverse(diag[0:1, cols], ups[0:1, cols], bx))
        xh_ref[b] = high
        xl_ref[b] = low
        xp_ref[0:1, cols] = jnp.exp(ups[0:1, cols] - ups_before[0:1, first:first + 1])
        xp_ref[1:2, cols] = jnp.exp(downs[0:1, last:last + 1] - downs_before[0:1, cols])

    def own(values, which, start):
        shift = lax.rem(length - start, length)
        return pltpu.roll(values, shift, 1)[which:which + 1]

    def passes(which, start, count):
        u0, d0 = own(ups_before, which, start)[:, 0:1], own(downs_before, which, start)
        u1, d1 = own(ups, which, start), own(downs, which, start)[:, count - 1:count]
        return u1, u0, d1, jnp.exp(jnp.minimum(u1 - u0, 0.0)), jnp.exp(jnp.minimum(d1 - d0, 0.0))

    wide = -(-yc // 128) * 128
    y0 = row * yc
    sums, up_first, down_last, onward, backward = passes(1, y0, yc)
    block = block_of_inverse(own(diag, 1, y0)[:, :wide], sums[:, :wide], wide)[:yc, :yc]
    high = block.astype(jnp.bfloat16).astype(jnp.float32)
    ym_ref[:, 0:yc] = high
    ym_ref[:, yc:2 * yc] = high
    ym_ref[:, 2 * yc:3 * yc] = block - high
    lines = [onward, backward, own(faces, 1, y0), own(next_faces, 1, y0)]
    lines = [a[:, :wide] for a in lines] + [jnp.zeros((124, wide), jnp.float32)]
    yt_ref[...] = jnp.transpose(jnp.concatenate(lines, axis=0))[:yc]

    lane = lax.broadcasted_iota(jnp.int32, (1, 128), 1)
    low_weights = high_weights = jnp.zeros((1, 128), jnp.float32)
    for other in range(nr):
        last, first = (other + 1) * yc - 1, other * yc
        value = jnp.exp(jnp.minimum(up_first - ups[1:2, last:last + 1], 0.0))
        low_weights = jnp.where(lane == other, value, low_weights)
        value = jnp.exp(jnp.minimum(downs_before[1:2, first:first + 1] - down_last, 0.0))
        high_weights = jnp.where(lane == other, value, high_weights)

    z0 = col * zc
    _, _, _, onward, backward = passes(2, z0, zc)
    at = lax.broadcasted_iota(jnp.int32, (1, length), 1)
    over = jnp.where(at == zc - 1, own(diag, 2, z0), own(inverse, 2, z0))
    into = jnp.where(at == 0, 0.0, own(here, 2, z0) * over)
    lines = [
        over, into, own(down, 2, z0), own(faces, 2, z0), own(next_faces, 2, z0), onward, backward,
    ]
    for k, line in enumerate(lines):
        zt_ref[k:k + 1] = line[:, :128]
    zt_ref[7:8] = low_weights
    zt_ref[8:9] = high_weights
    zt_ref[9:16] = jnp.zeros((7, 128), jnp.float32)
    fetch.wait()


def on_chip(*shape):
    return pltpu.VMEM(shape, jnp.float32)


def split(a):
    high = a.astype(jnp.bfloat16)
    return high, (a - high.astype(jnp.float32)).astype(jnp.bfloat16)


def dot(a, b):
    return jnp.dot(a, b, preferred_element_type=jnp.float32)


def sweep_kernel(
    planes, zt_ref, u_ref, zlo_ref, zhi_ref, ylo_ref, yhi_ref,
    rea_ref, yt_ref, xh_ref, xl_ref, xp_ref, ym_ref, v_ref, ye_ref, ze_ref,
):
    step, steps = pl.program_id(0), pl.num_programs(0)
    zc, yc, nx = u_ref.shape
    nb, bx = xh_ref.shape[0], xh_ref.shape[1]
    kx, kxn = xp_ref[2:3], xp_ref[3:4]
    ky, kyn = yt_ref[:, 2:3], yt_ref[:, 3:4]
    lane = lax.broadcasted_iota(jnp.int32, (yc, nx), 1)
    sub = lax.broadcasted_iota(jnp.int32, (yc, nx), 0)

    @pl.when(step == 0)
    def _():
        v_ref[0] = jnp.zeros((yc, nx), jnp.float32)

    below = jnp.where(step == 0, zlo_ref[0], u_ref[jnp.maximum(step * planes - 1, 0)])
    above_last = u_ref[jnp.minimum((step + 1) * planes, zc - 1)]
    above_last = jnp.where(step == steps - 1, zhi_ref[0], above_last)
    changes = []
    for p in range(planes):
        z = step * planes + p
        u = u_ref[z]
        above = u_ref[z + 1] if p + 1 < planes else above_last
        left = jnp.where(lane == 0, 0.0, pltpu.roll(u, 1, 1))
        right = pltpu.roll(u, nx - 1, 1)
        down = jnp.where(sub == 0, ylo_ref[p], pltpu.roll(u, 1, 0))
        upper = jnp.where(sub == yc - 1, yhi_ref[p], pltpu.roll(u, yc - 1, 0))
        total = kxn * (right - u) - kx * (u - left)
        total += kyn * (upper - u) - ky * (u - down)
        total += zt_ref[4, z] * (above - u) - zt_ref[3, z] * (u - below)
        total += rea_ref[p] * u * (1.0 - u * u)
        changes.append(STEP * total)
        below = u
    change = jnp.concatenate(changes, axis=0) if planes > 1 else changes[0]
    local = []
    for b in range(nb):
        high, low = split(change[:, b * bx:(b + 1) * bx])
        local.append(dot(high, xh_ref[b]) + (dot(high, xl_ref[b]) + dot(low, xh_ref[b])))
    rows = planes * yc
    from_left = [jnp.zeros((rows, 1), jnp.float32)]
    from_right = [jnp.zeros((rows, 1), jnp.float32)]
    for b in range(nb - 1):
        through = xp_ref[0:1, (b + 1) * bx - 1:(b + 1) * bx]
        from_left.append(from_left[-1] * through + local[b][:, bx - 1:bx])
        c = nb - 1 - b
        through = xp_ref[1:2, c * bx:c * bx + 1]
        from_right.append(from_right[-1] * through + local[c][:, 0:1])
    from_right.reverse()
    solved = jnp.concatenate(
        [
            local[b]
            + xp_ref[0:1, b * bx:(b + 1) * bx] * from_left[b]
            + xp_ref[1:2, b * bx:(b + 1) * bx] * from_right[b]
            for b in range(nb)
        ],
        axis=1,
    )
    carry = v_ref[jnp.maximum(step * planes - 1, 0)]
    for p in range(planes):
        z = step * planes + p
        high, low = split(solved[p * yc:(p + 1) * yc])
        w = dot(ym_ref[...].astype(jnp.bfloat16), jnp.concatenate([high, low, high], axis=0))
        carry = zt_ref[0, z] * w + zt_ref[1, z] * carry
        v_ref[z] = carry

    @pl.when(step == steps - 1)
    def _():
        wide = 256 if nx % 256 == 0 else nx
        for x in range(nx // wide):
            cols = slice(x * wide, (x + 1) * wide)
            top = v_ref[zc - 1, :, cols]
            ze_ref[1, :, cols] = top
            ye_ref[0, zc - 1:zc, cols] = top[0:1]
            ye_ref[1, zc - 1:zc, cols] = top[yc - 1:yc]

            def back(i, value):
                z = zc - 2 - i
                value = v_ref[z, :, cols] + zt_ref[2, z] * value
                v_ref[z, :, cols] = value
                ye_ref[0, pl.ds(z, 1), cols] = value[0:1]
                ye_ref[1, pl.ds(z, 1), cols] = value[yc - 1:yc]
                return value

            ze_ref[0, :, cols] = lax.fori_loop(0, zc - 1, back, top)


def exchange_kernel(
    nr, nc, chunks, zt_ref, yp_ref, ye_ref, ze_ref, sy_ref, sz_ref,
    ybuf, zbuf, zsend, ysend_sem, yrecv_sem, zsend_sem, zrecv_sem,
):
    row, col = lax.axis_index("row"), lax.axis_index("col")
    zc, nx = ye_ref.shape[1], ye_ref.shape[2]
    yc = ze_ref.shape[1]
    has_low, has_high = col > 0, col < nc - 1
    barrier = pltpu.get_barrier_semaphore()
    for other in range(nr):
        @pl.when(other != row)
        def _():
            pl.semaphore_signal(barrier, inc=1, device_id=(other, col), device_id_type=MESH)

    @pl.when(has_low)
    def _():
        pl.semaphore_signal(barrier, inc=1, device_id=(row, col - 1), device_id_type=MESH)

    @pl.when(has_high)
    def _():
        pl.semaphore_signal(barrier, inc=1, device_id=(row, col + 1), device_id_type=MESH)

    pl.semaphore_wait(barrier, nr - 1 + has_low.astype(jnp.int32) + has_high.astype(jnp.int32))

    def y_copy(side, other, slot):
        return pltpu.make_async_remote_copy(
            src_ref=ye_ref.at[1 - side],
            dst_ref=ybuf.at[side, slot],
            send_sem=ysend_sem.at[side, other],
            recv_sem=yrecv_sem.at[side, slot],
            device_id=(other, col),
            device_id_type=MESH,
        )

    for other in range(nr):
        @pl.when(other > row)
        def _():
            y_copy(0, other, row).start()

        @pl.when(other < row)
        def _():
            y_copy(1, other, row).start()

    sy_ref[...] = jnp.zeros_like(sy_ref)
    for other in range(nr):
        @pl.when(other < row)
        def _():
            y_copy(0, other, other).wait_recv()
            sy_ref[0] += zt_ref[7, other] * ybuf[0, other]

        @pl.when(other > row)
        def _():
            y_copy(1, other, other).wait_recv()
            sy_ref[1] += zt_ref[8, other] * ybuf[1, other]

    yb, ya = yp_ref[:, 0:1], yp_ref[:, 1:2]
    part = yc // chunks

    def z_copy(side, k):
        rows = pl.ds(k * part, part)
        return pltpu.make_async_remote_copy(
            src_ref=zsend.at[side, rows],
            dst_ref=zbuf.at[side, rows],
            send_sem=zsend_sem.at[side, k],
            recv_sem=zrecv_sem.at[side, k],
            device_id=(row, col + (1 - 2 * side)),
            device_id_type=MESH,
        )

    def scan(side):
        source, target = (has_low, has_high) if side == 0 else (has_high, has_low)
        edge, z = (1, zc - 1) if side == 0 else (0, 0)
        through = zt_ref[5 + side, z]
        for k in range(chunks):
            rows = slice(k * part, (k + 1) * part)

            @pl.when(source)
            def _():
                z_copy(side, k).wait_recv()
                sz_ref[side, rows] = zbuf[side, rows]

            @pl.when(jnp.logical_not(source))
            def _():
                sz_ref[side, rows] = jnp.zeros((part, nx), jnp.float32)

            @pl.when(target)
            def _():
                value = ze_ref[edge, rows] + yb[rows] * sy_ref[0, z:z + 1]
                value += ya[rows] * sy_ref[1, z:z + 1]
                zsend[side, rows] = value + through * sz_ref[side, rows]
                z_copy(side, k).start()

    low_half = col < nc // 2

    @pl.when(low_half)
    def _():
        scan(0)

    scan(1)

    @pl.when(jnp.logical_not(low_half))
    def _():
        scan(0)

    for k in range(chunks):
        @pl.when(has_high)
        def _():
            z_copy(0, k).wait_send()

        @pl.when(has_low)
        def _():
            z_copy(1, k).wait_send()

    for other in range(nr):
        @pl.when(other > row)
        def _():
            y_copy(0, other, row).wait_send()

        @pl.when(other < row)
        def _():
            y_copy(1, other, row).wait_send()


def finish_kernel(planes, zt_ref, u_ref, v_ref, yp_ref, sy_ref, sz_ref, out_ref):
    yb, ya = yp_ref[:, 0:1], yp_ref[:, 1:2]
    for p in range(planes):
        z = pl.program_id(0) * planes + p
        value = u_ref[z] + v_ref[z]
        value += yb * sy_ref[0, pl.ds(z, 1)] + ya * sy_ref[1, pl.ds(z, 1)]
        out_ref[p] = value + zt_ref[5, z] * sz_ref[0] + zt_ref[6, z] * sz_ref[1]


def body(u, reaction, x_faces, y_faces, z_faces, x_inverse, y_inverse, z_inverse):
    zc, yc, nx = u.shape
    nr, nc = lax.axis_size("row"), lax.axis_size("col")
    row, col = lax.axis_index("row"), lax.axis_index("col")
    ny, nz = y_faces.shape[0], z_faces.shape[0]
    f32 = jnp.float32

    def up(n):
        return [(i, i + 1) for i in range(n - 1)]

    def down(n):
        return [(i + 1, i) for i in range(n - 1)]

    ylo = lax.ppermute(u[:, yc - 1:yc], "row", up(nr))
    yhi = lax.ppermute(u[:, 0:1], "row", down(nr))
    zlo = lax.ppermute(u[zc - 1:zc], "col", up(nc))
    zhi = lax.ppermute(u[0:1], "col", down(nc))

    longest = -(-max(nx, ny, nz) // 128) * 128
    faces = jnp.stack([jnp.pad(f, (0, longest - f.shape[0])) for f in (x_faces, y_faces, z_faces)])
    faces = jnp.pad(faces, ((0, 5), (0, 0)))
    pos = jnp.stack([row, col]).astype(jnp.int32)
    bx = 256 if nx % 256 == 0 else nx
    nb = nx // bx
    smem = pl.BlockSpec(memory_space=pltpu.SMEM)
    vmem = pl.BlockSpec(memory_space=pltpu.VMEM)
    xh, xl, xp, ym, yt, zt, held = pl.pallas_call(
        functools.partial(table_kernel, nr, zc, yc),
        in_specs=[smem, vmem, pl.BlockSpec(memory_space=pltpu.HBM)],
        out_specs=[vmem] * 7,
        out_shape=[
            jax.ShapeDtypeStruct((nb, bx, bx), jnp.bfloat16),
            jax.ShapeDtypeStruct((nb, bx, bx), jnp.bfloat16),
            jax.ShapeDtypeStruct((4, nx), f32),
            jax.ShapeDtypeStruct((yc, 3 * yc), f32),
            jax.ShapeDtypeStruct((yc, 128), f32),
            jax.ShapeDtypeStruct((16, 128), f32),
            on_chip(zc, yc, nx),
        ],
        scratch_shapes=[pltpu.SemaphoreType.DMA(())],
        compiler_params=pltpu.CompilerParams(vmem_limit_bytes=VMEM_LIMIT),
        cost_estimate=pl.CostEstimate(flops=40000000, bytes_accessed=1 << 20, transcendentals=0),
    )(pos, faces, u)

    planes = 2 if zc % 2 == 0 else 1
    steps = zc // planes
    reaction = pltpu.with_memory_space_constraint(reaction, pltpu.HBM)
    plane = (1, yc, nx)

    def whole(*shape):
        return pl.BlockSpec(shape, lambda s: (0,) * len(shape))

    slab = pl.BlockSpec((planes, yc, nx), lambda s: (s, 0, 0))
    line = pl.BlockSpec((planes, 1, nx), lambda s: (s, 0, 0))
    v, ye, ze = pl.pallas_call(
        functools.partial(sweep_kernel, planes),
        grid=(steps,),
        in_specs=[
            smem, vmem, whole(*plane), whole(*plane), line, line, slab,
            whole(yc, 128), whole(nb, bx, bx), whole(nb, bx, bx), whole(4, nx), whole(yc, 3 * yc),
        ],
        out_specs=[vmem, whole(2, zc, nx), whole(2, yc, nx)],
        out_shape=[
            on_chip(zc, yc, nx),
            jax.ShapeDtypeStruct((2, zc, nx), f32),
            jax.ShapeDtypeStruct((2, yc, nx), f32),
        ],
        compiler_params=pltpu.CompilerParams(vmem_limit_bytes=VMEM_LIMIT),
    )(zt, held, zlo, zhi, ylo, yhi, reaction, yt, xh, xl, xp, ym)

    chunks = 4 if yc % 32 == 0 else 1
    sy, sz = pl.pallas_call(
        functools.partial(exchange_kernel, nr, nc, chunks),
        in_specs=[smem, vmem, vmem, vmem],
        out_specs=[vmem, vmem],
        out_shape=[
            jax.ShapeDtypeStruct((2, zc, nx), f32),
            jax.ShapeDtypeStruct((2, yc, nx), f32),
        ],
        scratch_shapes=[
            pltpu.VMEM((2, nr, zc, nx), f32),
            pltpu.VMEM((2, yc, nx), f32),
            pltpu.VMEM((2, yc, nx), f32),
            pltpu.SemaphoreType.DMA((2, nr)),
            pltpu.SemaphoreType.DMA((2, nr)),
            pltpu.SemaphoreType.DMA((2, chunks)),
            pltpu.SemaphoreType.DMA((2, chunks)),
        ],
        compiler_params=pltpu.CompilerParams(
            collective_id=0, has_side_effects=True, vmem_limit_bytes=VMEM_LIMIT
        ),
    )(zt, yt, ye, ze)

    return pl.pallas_call(
        functools.partial(finish_kernel, planes),
        grid=(steps,),
        in_specs=[smem, vmem, vmem, whole(yc, 128), whole(2, zc, nx), whole(2, yc, nx)],
        out_specs=slab,
        out_shape=jax.ShapeDtypeStruct((zc, yc, nx), f32),
        compiler_params=pltpu.CompilerParams(vmem_limit_bytes=VMEM_LIMIT),
    )(zt, held, v, yt, sy, sz)


def solution(mesh):
    in_specs = (P("col", "row", None), P("col", "row", None), P(), P(), P(), P(), P(), P())
    out_specs = P("col", "row", None)
    return jax.shard_map(body, mesh=mesh, in_specs=in_specs, out_specs=out_specs, check_vma=False)
```

```python
import functools

import jax
import jax.numpy as jnp
from jax import lax
from jax.experimental import pallas as pl
from jax.experimental.pallas import tpu as pltpu
from jax.sharding import PartitionSpec as P

WEIGHT = 0.5
STEP = 1000.0
MESH = pl.DeviceIdType.MESH
VMEM_LIMIT = 24 * 1024 * 1024


def shifted(a, by, fill):
    n = a.shape[1]
    lane = lax.broadcasted_iota(jnp.int32, a.shape, 1)
    if by > 0:
        return jnp.where(lane >= by, pltpu.roll(a, by, 1), fill)
    return jnp.where(lane < n + by, pltpu.roll(a, n + by, 1), fill)


def running_sum(a):
    by = 1
    while by < a.shape[1]:
        a = a + shifted(a, by, 0.0)
        by *= 2
    return a


def ladder(couple, sign):
    p00, p01, p10, p11 = 1.0 + couple, couple, jnp.ones_like(couple), couple
    by = 1
    while by < couple.shape[1]:
        q00, q01 = shifted(p00, sign * by, 1.0), shifted(p01, sign * by, 0.0)
        q10, q11 = shifted(p10, sign * by, 0.0), shifted(p11, sign * by, 1.0)
        n00, n01 = p00 * q00 + p01 * q10, p00 * q01 + p01 * q11
        n10, n11 = p10 * q00 + p11 * q10, p10 * q01 + p11 * q11
        scale = 1.0 / (n00 + n01 + n10 + n11)
        p00, p01, p10, p11 = n00 * scale, n01 * scale, n10 * scale, n11 * scale
        by *= 2
    return p00 / p10


def as_column(line, rows):
    n = line.shape[1]
    return jnp.transpose(jnp.broadcast_to(line, (n, n)))[:rows, :rows]


def block_of_inverse(diagonal, sums, n):
    i = lax.broadcasted_iota(jnp.int32, (n, n), 0)
    j = lax.broadcasted_iota(jnp.int32, (n, n), 1)
    near = jnp.where(i >= j, diagonal[:, :n], as_column(diagonal, n))
    return near * jnp.exp(-jnp.abs(as_column(sums, n) - sums[:, :n]))


def table_kernel(
    nr, nc, faces_ref, field_ref, xh_ref, xl_ref, xp_ref, ym_ref, yt_ref, zt_ref,
    held_ref, yhalo_ref, zhalo_ref, strips, edges, fetch_sem, strip_sem, send_sem, recv_sem,
):
    row, col = lax.axis_index("row"), lax.axis_index("col")
    zc, yc, _ = field_ref.shape
    tall = strips.shape[2]
    strip_copies = [
        pltpu.make_async_copy(
            field_ref.at[:, pl.ds(start, tall)], strips.at[side], strip_sem.at[side]
        )
        for side, start in ((0, yc - tall), (1, 0))
    ]
    for copy in strip_copies:
        copy.start()
    fetch = pltpu.make_async_copy(field_ref, held_ref, fetch_sem)
    fetch.start()
    places = [
        (row < nr - 1, row > 0, (row + 1, col)),
        (row > 0, row < nr - 1, (row - 1, col)),
        (col < nc - 1, col > 0, (row, col + 1)),
        (col > 0, col < nc - 1, (row, col - 1)),
    ]
    barrier = pltpu.get_barrier_semaphore()
    expected = 0
    for to, _, device in places:
        expected += to.astype(jnp.int32)

        @pl.when(to)
        def _():
            pl.semaphore_signal(barrier, inc=1, device_id=device, device_id_type=MESH)

    pl.semaphore_wait(barrier, expected)
    ends = [
        (edges.at[0], yhalo_ref.at[0]),
        (edges.at[1], yhalo_ref.at[1]),
        (field_ref.at[zc - 1], zhalo_ref.at[0]),
        (field_ref.at[0], zhalo_ref.at[1]),
    ]
    halo = [
        pltpu.make_async_remote_copy(
            src_ref=source, dst_ref=target, send_sem=send_sem.at[k], recv_sem=recv_sem.at[k],
            device_id=places[k][2], device_id_type=MESH,
        )
        for k, (source, target) in enumerate(ends)
    ]
    for k in (2, 3):
        @pl.when(places[k][0])
        def _():
            halo[k].start()

    for side in (0, 1):
        strip_copies[side].wait()
        for z in range(zc):
            at = tall - 1 if side == 0 else 0
            edges[side, z:z + 1] = strips[side, z, at:at + 1]

        @pl.when(places[side][0])
        def _():
            halo[side].start()

    for k in range(4):
        @pl.when(jnp.logical_not(places[k][1]))
        def _():
            target = ends[k][1]
            target[...] = jnp.zeros_like(target)

    faces = faces_ref[...]
    length = faces.shape[1]
    nb, bx = xh_ref.shape[0], xh_ref.shape[1]
    nx = nb * bx
    here = WEIGHT * STEP * faces
    above = shifted(here, -1, 0.0)
    e = ladder(here, 1)
    h = ladder(above, -1)
    pivot = above + e
    down = above / pivot
    inverse = 1.0 / pivot
    diag = 1.0 / (e + h - 1.0)
    ups = running_sum(jnp.log(jnp.maximum(here / (here + h), 1e-30)))
    downs = running_sum(jnp.log(jnp.maximum(down, 1e-30)))
    ups_before, downs_before = shifted(ups, 1, 0.0), shifted(downs, 1, 0.0)
    next_faces = shifted(faces, -1, 0.0)

    xp_ref[2:3] = faces[0:1, :nx]
    xp_ref[3:4] = next_faces[0:1, :nx]
    for b in range(nb):
        first, last = b * bx, (b + 1) * bx - 1
        cols = slice(first, last + 1)
        high, low = split(block_of_inverse(diag[0:1, cols], ups[0:1, cols], bx))
        xh_ref[b] = high
        xl_ref[b] = low
        xp_ref[0:1, cols] = jnp.exp(ups[0:1, cols] - ups_before[0:1, first:first + 1])
        xp_ref[1:2, cols] = jnp.exp(downs[0:1, last:last + 1] - downs_before[0:1, cols])

    def own(values, which, start):
        shift = lax.rem(length - start, length)
        return pltpu.roll(values, shift, 1)[which:which + 1]

    def passes(which, start, count):
        u0, d0 = own(ups_before, which, start)[:, 0:1], own(downs_before, which, start)
        u1, d1 = own(ups, which, start), own(downs, which, start)[:, count - 1:count]
        return u1, u0, d1, jnp.exp(jnp.minimum(u1 - u0, 0.0)), jnp.exp(jnp.minimum(d1 - d0, 0.0))

    wide = -(-yc // 128) * 128
    y0 = row * yc
    sums, up_first, down_last, onward, backward = passes(1, y0, yc)
    block = block_of_inverse(own(diag, 1, y0)[:, :wide], sums[:, :wide], wide)[:yc, :yc]
    high = block.astype(jnp.bfloat16).astype(jnp.float32)
    ym_ref[:, 0:yc] = high
    ym_ref[:, yc:2 * yc] = high
    ym_ref[:, 2 * yc:3 * yc] = block - high
    lines = [onward, backward, own(faces, 1, y0), own(next_faces, 1, y0)]
    lines = [a[:, :wide] for a in lines] + [jnp.zeros((124, wide), jnp.float32)]
    yt_ref[...] = jnp.transpose(jnp.concatenate(lines, axis=0))[:yc]

    lane = lax.broadcasted_iota(jnp.int32, (1, 128), 1)
    low_weights = high_weights = jnp.zeros((1, 128), jnp.float32)
    for other in range(nr):
        last, first = (other + 1) * yc - 1, other * yc
        value = jnp.exp(jnp.minimum(up_first - ups[1:2, last:last + 1], 0.0))
        low_weights = jnp.where(lane == other, value, low_weights)
        value = jnp.exp(jnp.minimum(downs_before[1:2, first:first + 1] - down_last, 0.0))
        high_weights = jnp.where(lane == other, value, high_weights)

    z0 = col * zc
    _, _, _, onward, backward = passes(2, z0, zc)
    at = lax.broadcasted_iota(jnp.int32, (1, length), 1)
    over = jnp.where(at == zc - 1, own(diag, 2, z0), own(inverse, 2, z0))
    into = jnp.where(at == 0, 0.0, own(here, 2, z0) * over)
    lines = [
        over, into, own(down, 2, z0), own(faces, 2, z0), own(next_faces, 2, z0), onward, backward,
    ]
    for k, line in enumerate(lines):
        zt_ref[k:k + 1] = line[:, :128]
    zt_ref[7:8] = low_weights
    zt_ref[8:9] = high_weights
    zt_ref[9:16] = jnp.zeros((7, 128), jnp.float32)
    for k in range(4):
        @pl.when(places[k][0])
        def _():
            halo[k].wait_send()

        @pl.when(places[k][1])
        def _():
            halo[k].wait_recv()

    fetch.wait()


def on_chip(*shape):
    return pltpu.VMEM(shape, jnp.float32)


def split(a):
    high = a.astype(jnp.bfloat16)
    return high, (a - high.astype(jnp.float32)).astype(jnp.bfloat16)


def dot(a, b):
    return jnp.dot(a, b, preferred_element_type=jnp.float32)


def sweep_kernel(
    planes, zt_ref, u_ref, yhalo_ref, zhalo_ref,
    rea_ref, yt_ref, xh_ref, xl_ref, xp_ref, ym_ref, v_ref, ye_ref, ze_ref,
):
    step, steps = pl.program_id(0), pl.num_programs(0)
    zc, yc, nx = u_ref.shape
    nb, bx = xh_ref.shape[0], xh_ref.shape[1]
    kx, kxn = xp_ref[2:3], xp_ref[3:4]
    ky, kyn = yt_ref[:, 2:3], yt_ref[:, 3:4]
    lane = lax.broadcasted_iota(jnp.int32, (yc, nx), 1)
    sub = lax.broadcasted_iota(jnp.int32, (yc, nx), 0)

    @pl.when(step == 0)
    def _():
        v_ref[0] = jnp.zeros((yc, nx), jnp.float32)

    below = jnp.where(step == 0, zhalo_ref[0], u_ref[jnp.maximum(step * planes - 1, 0)])
    above_last = u_ref[jnp.minimum((step + 1) * planes, zc - 1)]
    above_last = jnp.where(step == steps - 1, zhalo_ref[1], above_last)
    changes = []
    for p in range(planes):
        z = step * planes + p
        u = u_ref[z]
        above = u_ref[z + 1] if p + 1 < planes else above_last
        left = jnp.where(lane == 0, 0.0, pltpu.roll(u, 1, 1))
        right = pltpu.roll(u, nx - 1, 1)
        down = jnp.where(sub == 0, yhalo_ref[0, pl.ds(z, 1)], pltpu.roll(u, 1, 0))
        upper = jnp.where(sub == yc - 1, yhalo_ref[1, pl.ds(z, 1)], pltpu.roll(u, yc - 1, 0))
        total = kxn * (right - u) - kx * (u - left)
        total += kyn * (upper - u) - ky * (u - down)
        total += zt_ref[4, z] * (above - u) - zt_ref[3, z] * (u - below)
        total += rea_ref[p] * u * (1.0 - u * u)
        changes.append(STEP * total)
        below = u
    change = jnp.concatenate(changes, axis=0) if planes > 1 else changes[0]
    local = []
    for b in range(nb):
        high, low = split(change[:, b * bx:(b + 1) * bx])
        local.append(dot(high, xh_ref[b]) + (dot(high, xl_ref[b]) + dot(low, xh_ref[b])))
    rows = planes * yc
    from_left = [jnp.zeros((rows, 1), jnp.float32)]
    from_right = [jnp.zeros((rows, 1), jnp.float32)]
    for b in range(nb - 1):
        through = xp_ref[0:1, (b + 1) * bx - 1:(b + 1) * bx]
        from_left.append(from_left[-1] * through + local[b][:, bx - 1:bx])
        c = nb - 1 - b
        through = xp_ref[1:2, c * bx:c * bx + 1]
        from_right.append(from_right[-1] * through + local[c][:, 0:1])
    from_right.reverse()
    solved = jnp.concatenate(
        [
            local[b]
            + xp_ref[0:1, b * bx:(b + 1) * bx] * from_left[b]
            + xp_ref[1:2, b * bx:(b + 1) * bx] * from_right[b]
            for b in range(nb)
        ],
        axis=1,
    )
    carry = v_ref[jnp.maximum(step * planes - 1, 0)]
    for p in range(planes):
        z = step * planes + p
        high, low = split(solved[p * yc:(p + 1) * yc])
        w = dot(ym_ref[...].astype(jnp.bfloat16), jnp.concatenate([high, low, high], axis=0))
        carry = zt_ref[0, z] * w + zt_ref[1, z] * carry
        v_ref[z] = carry

    @pl.when(step == steps - 1)
    def _():
        wide = 256 if nx % 256 == 0 else nx
        for x in range(nx // wide):
            cols = slice(x * wide, (x + 1) * wide)
            top = v_ref[zc - 1, :, cols]
            ze_ref[1, :, cols] = top
            ye_ref[0, zc - 1:zc, cols] = top[0:1]
            ye_ref[1, zc - 1:zc, cols] = top[yc - 1:yc]

            def back(i, value):
                z = zc - 2 - i
                value = v_ref[z, :, cols] + zt_ref[2, z] * value
                v_ref[z, :, cols] = value
                ye_ref[0, pl.ds(z, 1), cols] = value[0:1]
                ye_ref[1, pl.ds(z, 1), cols] = value[yc - 1:yc]
                return value

            ze_ref[0, :, cols] = lax.fori_loop(0, zc - 1, back, top)


def exchange_kernel(
    nr, nc, chunks, zt_ref, yp_ref, ye_ref, ze_ref, sy_ref, sz_ref,
    ybuf, zbuf, zsend, esend, ebuf, ysend_sem, yrecv_sem, zsend_sem, zrecv_sem,
    esend_sem, erecv_sem,
):
    row, col = lax.axis_index("row"), lax.axis_index("col")
    zc, nx = ye_ref.shape[1], ye_ref.shape[2]
    yc = ze_ref.shape[1]
    has_low, has_high = col > 0, col < nc - 1
    barrier = pltpu.get_barrier_semaphore()
    for other in range(nr):
        @pl.when(other != row)
        def _():
            pl.semaphore_signal(barrier, inc=1, device_id=(other, col), device_id_type=MESH)

    @pl.when(has_low)
    def _():
        pl.semaphore_signal(barrier, inc=1, device_id=(row, col - 1), device_id_type=MESH)

    @pl.when(has_high)
    def _():
        pl.semaphore_signal(barrier, inc=1, device_id=(row, col + 1), device_id_type=MESH)

    pl.semaphore_wait(barrier, nr - 1 + has_low.astype(jnp.int32) + has_high.astype(jnp.int32))

    def y_copy(side, other, slot):
        return pltpu.make_async_remote_copy(
            src_ref=ye_ref.at[1 - side],
            dst_ref=ybuf.at[side, slot],
            send_sem=ysend_sem.at[side, other],
            recv_sem=yrecv_sem.at[side, slot],
            device_id=(other, col),
            device_id_type=MESH,
        )

    for other in range(nr):
        @pl.when(other > row)
        def _():
            y_copy(0, other, row).start()

        @pl.when(other < row)
        def _():
            y_copy(1, other, row).start()

    part = yc // chunks

    def z_copy(side, k):
        rows = pl.ds(k * part, part)
        return pltpu.make_async_remote_copy(
            src_ref=zsend.at[side, rows],
            dst_ref=zbuf.at[side, rows],
            send_sem=zsend_sem.at[side, k],
            recv_sem=zrecv_sem.at[side, k],
            device_id=(row, col + (1 - 2 * side)),
            device_id_type=MESH,
        )

    def scan(side):
        source, target = (has_low, has_high) if side == 0 else (has_high, has_low)
        edge, z = (1, zc - 1) if side == 0 else (0, 0)
        through = zt_ref[5 + side, z]
        for k in range(chunks):
            rows = slice(k * part, (k + 1) * part)

            @pl.when(source)
            def _():
                z_copy(side, k).wait_recv()
                sz_ref[side, rows] = zbuf[side, rows]

            @pl.when(jnp.logical_not(source))
            def _():
                sz_ref[side, rows] = jnp.zeros((part, nx), jnp.float32)

            @pl.when(target)
            def _():
                zsend[side, rows] = ze_ref[edge, rows] + through * sz_ref[side, rows]
                z_copy(side, k).start()

    low_half = col < nc // 2

    @pl.when(low_half)
    def _():
        scan(0)

    scan(1)

    @pl.when(jnp.logical_not(low_half))
    def _():
        scan(0)

    for k in range(2):
        esend[0, k:k + 1] = sz_ref[k, yc - 1:yc]
        esend[1, k:k + 1] = sz_ref[k, 0:1]

    def e_copy(side, other, slot):
        return pltpu.make_async_remote_copy(
            src_ref=esend.at[side],
            dst_ref=ebuf.at[side, slot],
            send_sem=esend_sem.at[side, other],
            recv_sem=erecv_sem.at[side, slot],
            device_id=(other, col),
            device_id_type=MESH,
        )

    for other in range(nr):
        @pl.when(other > row)
        def _():
            e_copy(0, other, row).start()

        @pl.when(other < row)
        def _():
            e_copy(1, other, row).start()

    sy_ref[...] = jnp.zeros_like(sy_ref)
    for other in range(nr):
        @pl.when(other < row)
        def _():
            y_copy(0, other, other).wait_recv()
            sy_ref[0] += zt_ref[7, other] * ybuf[0, other]

        @pl.when(other > row)
        def _():
            y_copy(1, other, other).wait_recv()
            sy_ref[1] += zt_ref[8, other] * ybuf[1, other]

    for other in range(nr):
        for side, here in ((0, other < row), (1, other > row)):
            @pl.when(here)
            def _():
                e_copy(side, other, other).wait_recv()
                coefficients = zt_ref[7 + side, other] * yp_ref[:, side:side + 1]
                for k in range(2):
                    sz_ref[k] += coefficients * ebuf[side, other, k:k + 1]

    for k in range(chunks):
        @pl.when(has_high)
        def _():
            z_copy(0, k).wait_send()

        @pl.when(has_low)
        def _():
            z_copy(1, k).wait_send()

    for other in range(nr):
        for side, there in ((0, other > row), (1, other < row)):
            @pl.when(there)
            def _():
                y_copy(side, other, row).wait_send()
                e_copy(side, other, row).wait_send()


def finish_kernel(planes, zt_ref, u_ref, v_ref, yp_ref, sy_ref, sz_ref, out_ref):
    yb, ya = yp_ref[:, 0:1], yp_ref[:, 1:2]
    for p in range(planes):
        z = pl.program_id(0) * planes + p
        value = u_ref[z] + v_ref[z]
        value += yb * sy_ref[0, pl.ds(z, 1)] + ya * sy_ref[1, pl.ds(z, 1)]
        out_ref[p] = value + zt_ref[5, z] * sz_ref[0] + zt_ref[6, z] * sz_ref[1]


def body(u, reaction, x_faces, y_faces, z_faces, x_inverse, y_inverse, z_inverse):
    zc, yc, nx = u.shape
    nr, nc = lax.axis_size("row"), lax.axis_size("col")
    ny, nz = y_faces.shape[0], z_faces.shape[0]
    f32 = jnp.float32

    longest = -(-max(nx, ny, nz) // 128) * 128
    faces = jnp.stack([jnp.pad(f, (0, longest - f.shape[0])) for f in (x_faces, y_faces, z_faces)])
    faces = jnp.pad(faces, ((0, 5), (0, 0)))
    tall = 8 if yc % 8 == 0 else yc
    bx = 256 if nx % 256 == 0 else nx
    nb = nx // bx
    smem = pl.BlockSpec(memory_space=pltpu.SMEM)
    vmem = pl.BlockSpec(memory_space=pltpu.VMEM)
    xh, xl, xp, ym, yt, zt, held, yhalo, zhalo = pl.pallas_call(
        functools.partial(table_kernel, nr, nc),
        in_specs=[vmem, pl.BlockSpec(memory_space=pltpu.HBM)],
        out_specs=[vmem] * 9,
        out_shape=[
            jax.ShapeDtypeStruct((nb, bx, bx), jnp.bfloat16),
            jax.ShapeDtypeStruct((nb, bx, bx), jnp.bfloat16),
            jax.ShapeDtypeStruct((4, nx), f32),
            jax.ShapeDtypeStruct((yc, 3 * yc), f32),
            jax.ShapeDtypeStruct((yc, 128), f32),
            jax.ShapeDtypeStruct((16, 128), f32),
            on_chip(zc, yc, nx),
            on_chip(2, zc, nx),
            on_chip(2, yc, nx),
        ],
        scratch_shapes=[
            pltpu.VMEM((2, zc, tall, nx), f32),
            pltpu.VMEM((2, zc, nx), f32),
            pltpu.SemaphoreType.DMA(()),
            pltpu.SemaphoreType.DMA((2,)),
            pltpu.SemaphoreType.DMA((4,)),
            pltpu.SemaphoreType.DMA((4,)),
        ],
        compiler_params=pltpu.CompilerParams(
            collective_id=1, has_side_effects=True, vmem_limit_bytes=VMEM_LIMIT
        ),
        cost_estimate=pl.CostEstimate(flops=40000000, bytes_accessed=1 << 20, transcendentals=0),
    )(faces, pltpu.with_memory_space_constraint(u, pltpu.HBM))

    planes = 2 if zc % 2 == 0 else 1
    steps = zc // planes
    reaction = pltpu.with_memory_space_constraint(reaction, pltpu.HBM)

    def whole(*shape):
        return pl.BlockSpec(shape, lambda s: (0,) * len(shape))

    slab = pl.BlockSpec((planes, yc, nx), lambda s: (s, 0, 0))
    v, ye, ze = pl.pallas_call(
        functools.partial(sweep_kernel, planes),
        grid=(steps,),
        in_specs=[
            smem, vmem, vmem, vmem, slab,
            whole(yc, 128), whole(nb, bx, bx), whole(nb, bx, bx), whole(4, nx), whole(yc, 3 * yc),
        ],
        out_specs=[vmem, whole(2, zc, nx), whole(2, yc, nx)],
        out_shape=[
            on_chip(zc, yc, nx),
            jax.ShapeDtypeStruct((2, zc, nx), f32),
            jax.ShapeDtypeStruct((2, yc, nx), f32),
        ],
        compiler_params=pltpu.CompilerParams(vmem_limit_bytes=VMEM_LIMIT),
    )(zt, held, yhalo, zhalo, reaction, yt, xh, xl, xp, ym)

    chunks = yc // 8 if yc % 8 == 0 else 1
    sy, sz = pl.pallas_call(
        functools.partial(exchange_kernel, nr, nc, chunks),
        in_specs=[smem, vmem, vmem, vmem],
        out_specs=[vmem, vmem],
        out_shape=[
            jax.ShapeDtypeStruct((2, zc, nx), f32),
            jax.ShapeDtypeStruct((2, yc, nx), f32),
        ],
        scratch_shapes=[
            pltpu.VMEM((2, nr, zc, nx), f32),
            pltpu.VMEM((2, yc, nx), f32),
            pltpu.VMEM((2, yc, nx), f32),
            pltpu.VMEM((2, 2, nx), f32),
            pltpu.VMEM((2, nr, 2, nx), f32),
            pltpu.SemaphoreType.DMA((2, nr)),
            pltpu.SemaphoreType.DMA((2, nr)),
            pltpu.SemaphoreType.DMA((2, chunks)),
            pltpu.SemaphoreType.DMA((2, chunks)),
            pltpu.SemaphoreType.DMA((2, nr)),
            pltpu.SemaphoreType.DMA((2, nr)),
        ],
        compiler_params=pltpu.CompilerParams(
            collective_id=0, has_side_effects=True, vmem_limit_bytes=VMEM_LIMIT
        ),
    )(zt, yt, ye, ze)

    return pl.pallas_call(
        functools.partial(finish_kernel, planes),
        grid=(steps,),
        in_specs=[smem, vmem, vmem, whole(yc, 128), whole(2, zc, nx), whole(2, yc, nx)],
        out_specs=slab,
        out_shape=jax.ShapeDtypeStruct((zc, yc, nx), f32),
        compiler_params=pltpu.CompilerParams(vmem_limit_bytes=VMEM_LIMIT),
    )(zt, held, v, yt, sy, sz)


def solution(mesh):
    in_specs = (P("col", "row", None), P("col", "row", None), P(), P(), P(), P(), P(), P())
    out_specs = P("col", "row", None)
    return jax.shard_map(body, mesh=mesh, in_specs=in_specs, out_specs=out_specs, check_vma=False)
```

```python
import functools

import jax
import jax.numpy as jnp
from jax import lax
from jax.experimental import pallas as pl
from jax.experimental.pallas import tpu as pltpu
from jax.sharding import PartitionSpec as P

WEIGHT = 0.5
STEP = 1000.0
MESH = pl.DeviceIdType.MESH
VMEM_LIMIT = 24 * 1024 * 1024


def shifted(a, by, fill):
    n = a.shape[1]
    lane = lax.broadcasted_iota(jnp.int32, a.shape, 1)
    if by > 0:
        return jnp.where(lane >= by, pltpu.roll(a, by, 1), fill)
    return jnp.where(lane < n + by, pltpu.roll(a, n + by, 1), fill)


def running_sum(a):
    by = 1
    while by < a.shape[1]:
        a = a + shifted(a, by, 0.0)
        by *= 2
    return a


def ladder(couple, sign):
    p00, p01, p10, p11 = 1.0 + couple, couple, jnp.ones_like(couple), couple
    by = 1
    while by < couple.shape[1]:
        q00, q01 = shifted(p00, sign * by, 1.0), shifted(p01, sign * by, 0.0)
        q10, q11 = shifted(p10, sign * by, 0.0), shifted(p11, sign * by, 1.0)
        n00, n01 = p00 * q00 + p01 * q10, p00 * q01 + p01 * q11
        n10, n11 = p10 * q00 + p11 * q10, p10 * q01 + p11 * q11
        scale = 1.0 / (n00 + n01 + n10 + n11)
        p00, p01, p10, p11 = n00 * scale, n01 * scale, n10 * scale, n11 * scale
        by *= 2
    return p00 / p10


def as_column(line, rows):
    n = line.shape[1]
    return jnp.transpose(jnp.broadcast_to(line, (n, n)))[:rows, :rows]


def block_of_inverse(diagonal, sums, n):
    i = lax.broadcasted_iota(jnp.int32, (n, n), 0)
    j = lax.broadcasted_iota(jnp.int32, (n, n), 1)
    near = jnp.where(i >= j, diagonal[:, :n], as_column(diagonal, n))
    return near * jnp.exp(-jnp.abs(as_column(sums, n) - sums[:, :n]))


def table_kernel(
    nr, nc, xf_ref, yf_ref, zf_ref, field_ref, xh_ref, xl_ref, xp_ref, ym_ref, yt_ref, zt_ref,
    held_ref, yhalo_ref, zhalo_ref, strips, edges, fetch_sem, strip_sem, send_sem, recv_sem,
):
    row, col = lax.axis_index("row"), lax.axis_index("col")
    zc, yc, _ = field_ref.shape
    tall = strips.shape[2]
    strip_copies = [
        pltpu.make_async_copy(
            field_ref.at[:, pl.ds(start, tall)], strips.at[side], strip_sem.at[side]
        )
        for side, start in ((0, yc - tall), (1, 0))
    ]
    for copy in strip_copies:
        copy.start()
    fetch = pltpu.make_async_copy(field_ref, held_ref, fetch_sem)
    fetch.start()
    places = [
        (row < nr - 1, row > 0, (row + 1, col)),
        (row > 0, row < nr - 1, (row - 1, col)),
        (col < nc - 1, col > 0, (row, col + 1)),
        (col > 0, col < nc - 1, (row, col - 1)),
    ]
    barrier = pltpu.get_barrier_semaphore()
    expected = 0
    for to, _, device in places:
        expected += to.astype(jnp.int32)

        @pl.when(to)
        def _():
            pl.semaphore_signal(barrier, inc=1, device_id=device, device_id_type=MESH)

    pl.semaphore_wait(barrier, expected)
    ends = [
        (edges.at[0], yhalo_ref.at[0]),
        (edges.at[1], yhalo_ref.at[1]),
        (field_ref.at[zc - 1], zhalo_ref.at[0]),
        (field_ref.at[0], zhalo_ref.at[1]),
    ]
    halo = [
        pltpu.make_async_remote_copy(
            src_ref=source, dst_ref=target, send_sem=send_sem.at[k], recv_sem=recv_sem.at[k],
            device_id=places[k][2], device_id_type=MESH,
        )
        for k, (source, target) in enumerate(ends)
    ]
    for k in (2, 3):
        @pl.when(places[k][0])
        def _():
            halo[k].start()

    for side in (0, 1):
        strip_copies[side].wait()
        for z in range(zc):
            at = tall - 1 if side == 0 else 0
            edges[side, z:z + 1] = strips[side, z, at:at + 1]

        @pl.when(places[side][0])
        def _():
            halo[side].start()

    for k in range(4):
        @pl.when(jnp.logical_not(places[k][1]))
        def _():
            target = ends[k][1]
            target[...] = jnp.zeros_like(target)

    given = [xf_ref[...], yf_ref[...], zf_ref[...]]
    length = -(-max(a.shape[1] for a in given) // 128) * 128
    lines = []
    for a in given:
        missing = length - a.shape[1]
        lines.append(jnp.concatenate([a, jnp.zeros((1, missing), a.dtype)], 1) if missing else a)
    faces = jnp.concatenate(lines + [jnp.zeros((5, length), jnp.float32)], axis=0)
    nb, bx = xh_ref.shape[0], xh_ref.shape[1]
    nx = nb * bx
    here = WEIGHT * STEP * faces
    above = shifted(here, -1, 0.0)
    e = ladder(here, 1)
    h = ladder(above, -1)
    pivot = above + e
    down = above / pivot
    inverse = 1.0 / pivot
    diag = 1.0 / (e + h - 1.0)
    ups = running_sum(jnp.log(jnp.maximum(here / (here + h), 1e-30)))
    downs = running_sum(jnp.log(jnp.maximum(down, 1e-30)))
    ups_before, downs_before = shifted(ups, 1, 0.0), shifted(downs, 1, 0.0)
    full, next_full = STEP * faces, STEP * shifted(faces, -1, 0.0)
    around = full + next_full

    xp_ref[2:3] = shifted(next_full, 1, 0.0)[0:1, :nx]
    xp_ref[3:4] = next_full[0:1, :nx]
    xp_ref[4:5] = around[0:1, :nx]
    for b in range(nb):
        first, last = b * bx, (b + 1) * bx - 1
        cols = slice(first, last + 1)
        high, low = split(block_of_inverse(diag[0:1, cols], ups[0:1, cols], bx))
        xh_ref[b] = high
        xl_ref[b] = low
        xp_ref[0:1, cols] = jnp.exp(ups[0:1, cols] - ups_before[0:1, first:first + 1])
        xp_ref[1:2, cols] = jnp.exp(downs[0:1, last:last + 1] - downs_before[0:1, cols])

    def own(values, which, start):
        shift = lax.rem(length - start, length)
        return pltpu.roll(values, shift, 1)[which:which + 1]

    def passes(which, start, count):
        u0, d0 = own(ups_before, which, start)[:, 0:1], own(downs_before, which, start)
        u1, d1 = own(ups, which, start), own(downs, which, start)[:, count - 1:count]
        return u1, u0, d1, jnp.exp(jnp.minimum(u1 - u0, 0.0)), jnp.exp(jnp.minimum(d1 - d0, 0.0))

    wide = -(-yc // 128) * 128
    y0 = row * yc
    sums, up_first, down_last, onward, backward = passes(1, y0, yc)
    block = block_of_inverse(own(diag, 1, y0)[:, :wide], sums[:, :wide], wide)[:yc, :yc]
    high = block.astype(jnp.bfloat16).astype(jnp.float32)
    ym_ref[:, 0:yc] = high
    ym_ref[:, yc:2 * yc] = high
    ym_ref[:, 2 * yc:3 * yc] = block - high
    lines = [onward, backward, own(full, 1, y0), own(next_full, 1, y0), own(around, 1, y0)]
    lines = [a[:, :wide] for a in lines] + [jnp.zeros((123, wide), jnp.float32)]
    yt_ref[...] = jnp.transpose(jnp.concatenate(lines, axis=0))[:yc]

    lane = lax.broadcasted_iota(jnp.int32, (1, 128), 1)
    low_weights = high_weights = jnp.zeros((1, 128), jnp.float32)
    for other in range(nr):
        last, first = (other + 1) * yc - 1, other * yc
        value = jnp.exp(jnp.minimum(up_first - ups[1:2, last:last + 1], 0.0))
        low_weights = jnp.where(lane == other, value, low_weights)
        value = jnp.exp(jnp.minimum(downs_before[1:2, first:first + 1] - down_last, 0.0))
        high_weights = jnp.where(lane == other, value, high_weights)

    z0 = col * zc
    _, _, _, onward, backward = passes(2, z0, zc)
    at = lax.broadcasted_iota(jnp.int32, (1, length), 1)
    over = jnp.where(at == zc - 1, own(diag, 2, z0), own(inverse, 2, z0))
    into = jnp.where(at == 0, 0.0, own(here, 2, z0) * over)
    lines = [
        over, into, own(down, 2, z0), own(full, 2, z0), own(next_full, 2, z0), onward, backward,
    ]
    for k, line in enumerate(lines):
        zt_ref[k:k + 1] = line[:, :128]
    zt_ref[7:8] = low_weights
    zt_ref[8:9] = high_weights
    zt_ref[9:10] = own(around, 2, z0)[:, :128]
    zt_ref[10:16] = jnp.zeros((6, 128), jnp.float32)
    for k in range(4):
        @pl.when(places[k][0])
        def _():
            halo[k].wait_send()

        @pl.when(places[k][1])
        def _():
            halo[k].wait_recv()

    fetch.wait()


def on_chip(*shape):
    return pltpu.VMEM(shape, jnp.float32)


def split(a):
    high = a.astype(jnp.bfloat16)
    return high, (a - high.astype(jnp.float32)).astype(jnp.bfloat16)


def dot(a, b):
    return jnp.dot(a, b, preferred_element_type=jnp.float32)


def sweep_kernel(
    planes, zt_ref, u_ref, yhalo_ref, zhalo_ref,
    rea_ref, yt_ref, xh_ref, xl_ref, xp_ref, ym_ref, v_ref, ye_ref, ze_ref,
):
    step, steps = pl.program_id(0), pl.num_programs(0)
    zc, yc, nx = u_ref.shape
    nb, bx = xh_ref.shape[0], xh_ref.shape[1]
    kx, kxn = xp_ref[2:3], xp_ref[3:4]
    ky, kyn = yt_ref[:, 2:3], yt_ref[:, 3:4]
    sub = lax.broadcasted_iota(jnp.int32, (yc, nx), 0)

    @pl.when(step == 0)
    def _():
        v_ref[0] = jnp.zeros((yc, nx), jnp.float32)

    below = jnp.where(step == 0, zhalo_ref[0], u_ref[jnp.maximum(step * planes - 1, 0)])
    above_last = u_ref[jnp.minimum((step + 1) * planes, zc - 1)]
    above_last = jnp.where(step == steps - 1, zhalo_ref[1], above_last)
    changes = []
    for p in range(planes):
        z = step * planes + p
        u = u_ref[z]
        above = u_ref[z + 1] if p + 1 < planes else above_last
        down = jnp.where(sub == 0, yhalo_ref[0, pl.ds(z, 1)], pltpu.roll(u, 1, 0))
        upper = jnp.where(sub == yc - 1, yhalo_ref[1, pl.ds(z, 1)], pltpu.roll(u, yc - 1, 0))
        total = kxn * pltpu.roll(u, nx - 1, 1) + kx * pltpu.roll(u, 1, 1)
        total += kyn * upper + ky * down
        total += zt_ref[4, z] * above + zt_ref[3, z] * below
        centre = STEP * rea_ref[p] * (1.0 - u * u) - (xp_ref[4:5] + (yt_ref[:, 4:5] + zt_ref[9, z]))
        changes.append(total + u * centre)
        below = u
    change = jnp.concatenate(changes, axis=0) if planes > 1 else changes[0]
    local = []
    for b in range(nb):
        high, low = split(change[:, b * bx:(b + 1) * bx])
        local.append(dot(high, xh_ref[b]) + (dot(high, xl_ref[b]) + dot(low, xh_ref[b])))
    rows = planes * yc
    from_left = [jnp.zeros((rows, 1), jnp.float32)]
    from_right = [jnp.zeros((rows, 1), jnp.float32)]
    for b in range(nb - 1):
        through = xp_ref[0:1, (b + 1) * bx - 1:(b + 1) * bx]
        from_left.append(from_left[-1] * through + local[b][:, bx - 1:bx])
        c = nb - 1 - b
        through = xp_ref[1:2, c * bx:c * bx + 1]
        from_right.append(from_right[-1] * through + local[c][:, 0:1])
    from_right.reverse()
    solved = jnp.concatenate(
        [
            local[b]
            + xp_ref[0:1, b * bx:(b + 1) * bx] * from_left[b]
            + xp_ref[1:2, b * bx:(b + 1) * bx] * from_right[b]
            for b in range(nb)
        ],
        axis=1,
    )
    carry = v_ref[jnp.maximum(step * planes - 1, 0)]
    for p in range(planes):
        z = step * planes + p
        high, low = split(solved[p * yc:(p + 1) * yc])
        w = dot(ym_ref[...].astype(jnp.bfloat16), jnp.concatenate([high, low, high], axis=0))
        carry = zt_ref[0, z] * w + zt_ref[1, z] * carry
        v_ref[z] = carry

    @pl.when(step == steps - 1)
    def _():
        wide = 256 if nx % 256 == 0 else nx
        for x in range(nx // wide):
            cols = slice(x * wide, (x + 1) * wide)
            top = v_ref[zc - 1, :, cols]
            ze_ref[1, :, cols] = top
            ye_ref[0, zc - 1:zc, cols] = top[0:1]
            ye_ref[1, zc - 1:zc, cols] = top[yc - 1:yc]

            def back(i, value):
                z = zc - 2 - i
                value = v_ref[z, :, cols] + zt_ref[2, z] * value
                v_ref[z, :, cols] = value
                ye_ref[0, pl.ds(z, 1), cols] = value[0:1]
                ye_ref[1, pl.ds(z, 1), cols] = value[yc - 1:yc]
                return value

            ze_ref[0, :, cols] = lax.fori_loop(0, zc - 1, back, top)


def exchange_kernel(
    nr, nc, chunks, zt_ref, yp_ref, ye_ref, ze_ref, sy_ref, sz_ref,
    ybuf, zbuf, zsend, esend, ebuf, ysend_sem, yrecv_sem, zsend_sem, zrecv_sem,
    esend_sem, erecv_sem,
):
    row, col = lax.axis_index("row"), lax.axis_index("col")
    zc, nx = ye_ref.shape[1], ye_ref.shape[2]
    yc = ze_ref.shape[1]
    has_low, has_high = col > 0, col < nc - 1
    barrier = pltpu.get_barrier_semaphore()
    for other in range(nr):
        @pl.when(other != row)
        def _():
            pl.semaphore_signal(barrier, inc=1, device_id=(other, col), device_id_type=MESH)

    @pl.when(has_low)
    def _():
        pl.semaphore_signal(barrier, inc=1, device_id=(row, col - 1), device_id_type=MESH)

    @pl.when(has_high)
    def _():
        pl.semaphore_signal(barrier, inc=1, device_id=(row, col + 1), device_id_type=MESH)

    pl.semaphore_wait(barrier, nr - 1 + has_low.astype(jnp.int32) + has_high.astype(jnp.int32))

    def y_copy(side, other, slot):
        return pltpu.make_async_remote_copy(
            src_ref=ye_ref.at[1 - side],
            dst_ref=ybuf.at[side, slot],
            send_sem=ysend_sem.at[side, other],
            recv_sem=yrecv_sem.at[side, slot],
            device_id=(other, col),
            device_id_type=MESH,
        )

    for other in range(nr):
        @pl.when(other > row)
        def _():
            y_copy(0, other, row).start()

        @pl.when(other < row)
        def _():
            y_copy(1, other, row).start()

    part = yc // chunks

    def z_copy(side, k):
        rows = pl.ds(k * part, part)
        return pltpu.make_async_remote_copy(
            src_ref=zsend.at[side, rows],
            dst_ref=zbuf.at[side, rows],
            send_sem=zsend_sem.at[side, k],
            recv_sem=zrecv_sem.at[side, k],
            device_id=(row, col + (1 - 2 * side)),
            device_id_type=MESH,
        )

    def scan(side):
        source, target = (has_low, has_high) if side == 0 else (has_high, has_low)
        edge, z = (1, zc - 1) if side == 0 else (0, 0)
        through = zt_ref[5 + side, z]
        for k in range(chunks):
            rows = slice(k * part, (k + 1) * part)

            @pl.when(source)
            def _():
                z_copy(side, k).wait_recv()
                sz_ref[side, rows] = zbuf[side, rows]

            @pl.when(jnp.logical_not(source))
            def _():
                sz_ref[side, rows] = jnp.zeros((part, nx), jnp.float32)

            @pl.when(target)
            def _():
                zsend[side, rows] = ze_ref[edge, rows] + through * sz_ref[side, rows]
                z_copy(side, k).start()

    low_half = col < nc // 2

    @pl.when(low_half)
    def _():
        scan(0)

    scan(1)

    @pl.when(jnp.logical_not(low_half))
    def _():
        scan(0)

    for k in range(2):
        esend[0, k:k + 1] = sz_ref[k, yc - 1:yc]
        esend[1, k:k + 1] = sz_ref[k, 0:1]

    def e_copy(side, other, slot):
        return pltpu.make_async_remote_copy(
            src_ref=esend.at[side],
            dst_ref=ebuf.at[side, slot],
            send_sem=esend_sem.at[side, other],
            recv_sem=erecv_sem.at[side, slot],
            device_id=(other, col),
            device_id_type=MESH,
        )

    for other in range(nr):
        @pl.when(other > row)
        def _():
            e_copy(0, other, row).start()

        @pl.when(other < row)
        def _():
            e_copy(1, other, row).start()

    sy_ref[...] = jnp.zeros_like(sy_ref)
    for other in range(nr):
        @pl.when(other < row)
        def _():
            y_copy(0, other, other).wait_recv()
            sy_ref[0] += zt_ref[7, other] * ybuf[0, other]

        @pl.when(other > row)
        def _():
            y_copy(1, other, other).wait_recv()
            sy_ref[1] += zt_ref[8, other] * ybuf[1, other]

    for other in range(nr):
        for side, here in ((0, other < row), (1, other > row)):
            @pl.when(here)
            def _():
                e_copy(side, other, other).wait_recv()
                coefficients = zt_ref[7 + side, other] * yp_ref[:, side:side + 1]
                for k in range(2):
                    sz_ref[k] += coefficients * ebuf[side, other, k:k + 1]

    for k in range(chunks):
        @pl.when(has_high)
        def _():
            z_copy(0, k).wait_send()

        @pl.when(has_low)
        def _():
            z_copy(1, k).wait_send()

    for other in range(nr):
        for side, there in ((0, other > row), (1, other < row)):
            @pl.when(there)
            def _():
                y_copy(side, other, row).wait_send()
                e_copy(side, other, row).wait_send()


def finish_kernel(planes, zt_ref, u_ref, v_ref, yp_ref, sy_ref, sz_ref, out_ref):
    yb, ya = yp_ref[:, 0:1], yp_ref[:, 1:2]
    for p in range(planes):
        z = pl.program_id(0) * planes + p
        value = u_ref[z] + v_ref[z]
        value += yb * sy_ref[0, pl.ds(z, 1)] + ya * sy_ref[1, pl.ds(z, 1)]
        out_ref[p] = value + zt_ref[5, z] * sz_ref[0] + zt_ref[6, z] * sz_ref[1]


def body(u, reaction, x_faces, y_faces, z_faces, x_inverse, y_inverse, z_inverse):
    zc, yc, nx = u.shape
    nr, nc = lax.axis_size("row"), lax.axis_size("col")
    f32 = jnp.float32

    tall = 8 if yc % 8 == 0 else yc
    bx = 256 if nx % 256 == 0 else nx
    nb = nx // bx
    smem = pl.BlockSpec(memory_space=pltpu.SMEM)
    vmem = pl.BlockSpec(memory_space=pltpu.VMEM)
    xh, xl, xp, ym, yt, zt, held, yhalo, zhalo = pl.pallas_call(
        functools.partial(table_kernel, nr, nc),
        in_specs=[vmem, vmem, vmem, pl.BlockSpec(memory_space=pltpu.HBM)],
        out_specs=[vmem] * 9,
        out_shape=[
            jax.ShapeDtypeStruct((nb, bx, bx), jnp.bfloat16),
            jax.ShapeDtypeStruct((nb, bx, bx), jnp.bfloat16),
            jax.ShapeDtypeStruct((8, nx), f32),
            jax.ShapeDtypeStruct((yc, 3 * yc), f32),
            jax.ShapeDtypeStruct((yc, 128), f32),
            jax.ShapeDtypeStruct((16, 128), f32),
            on_chip(zc, yc, nx),
            on_chip(2, zc, nx),
            on_chip(2, yc, nx),
        ],
        scratch_shapes=[
            pltpu.VMEM((2, zc, tall, nx), f32),
            pltpu.VMEM((2, zc, nx), f32),
            pltpu.SemaphoreType.DMA(()),
            pltpu.SemaphoreType.DMA((2,)),
            pltpu.SemaphoreType.DMA((4,)),
            pltpu.SemaphoreType.DMA((4,)),
        ],
        compiler_params=pltpu.CompilerParams(
            collective_id=1, has_side_effects=True, vmem_limit_bytes=VMEM_LIMIT
        ),
        cost_estimate=pl.CostEstimate(flops=40000000, bytes_accessed=1 << 20, transcendentals=0),
    )(x_faces[None], y_faces[None], z_faces[None], pltpu.with_memory_space_constraint(u, pltpu.HBM))

    planes = next(p for p in (4, 2, 1) if zc % p == 0)
    last = next(p for p in (8, 4, 2, 1) if zc % p == 0)
    reaction = pltpu.with_memory_space_constraint(reaction, pltpu.HBM)

    slab = pl.BlockSpec((planes, yc, nx), lambda step: (step, 0, 0))
    v, ye, ze = pl.pallas_call(
        functools.partial(sweep_kernel, planes),
        grid=(zc // planes,),
        in_specs=[
            smem, vmem, vmem, vmem, slab,
            vmem, vmem, vmem, vmem, vmem,
        ],
        out_specs=[vmem, vmem, vmem],
        out_shape=[
            on_chip(zc, yc, nx),
            jax.ShapeDtypeStruct((2, zc, nx), f32),
            jax.ShapeDtypeStruct((2, yc, nx), f32),
        ],
        compiler_params=pltpu.CompilerParams(vmem_limit_bytes=VMEM_LIMIT),
    )(zt, held, yhalo, zhalo, reaction, yt, xh, xl, xp, ym)

    chunks = yc // 8 if yc % 8 == 0 else 1
    sy, sz = pl.pallas_call(
        functools.partial(exchange_kernel, nr, nc, chunks),
        in_specs=[smem, vmem, vmem, vmem],
        out_specs=[vmem, vmem],
        out_shape=[
            jax.ShapeDtypeStruct((2, zc, nx), f32),
            jax.ShapeDtypeStruct((2, yc, nx), f32),
        ],
        scratch_shapes=[
            pltpu.VMEM((2, nr, zc, nx), f32),
            pltpu.VMEM((2, yc, nx), f32),
            pltpu.VMEM((2, yc, nx), f32),
            pltpu.VMEM((2, 2, nx), f32),
            pltpu.VMEM((2, nr, 2, nx), f32),
            pltpu.SemaphoreType.DMA((2, nr)),
            pltpu.SemaphoreType.DMA((2, nr)),
            pltpu.SemaphoreType.DMA((2, chunks)),
            pltpu.SemaphoreType.DMA((2, chunks)),
            pltpu.SemaphoreType.DMA((2, nr)),
            pltpu.SemaphoreType.DMA((2, nr)),
        ],
        compiler_params=pltpu.CompilerParams(
            collective_id=0, has_side_effects=True, vmem_limit_bytes=VMEM_LIMIT
        ),
    )(zt, yt, ye, ze)

    return pl.pallas_call(
        functools.partial(finish_kernel, last),
        grid=(zc // last,),
        in_specs=[smem, vmem, vmem, vmem, vmem, vmem],
        out_specs=pl.BlockSpec((last, yc, nx), lambda step: (step, 0, 0)),
        out_shape=jax.ShapeDtypeStruct((zc, yc, nx), f32),
        compiler_params=pltpu.CompilerParams(vmem_limit_bytes=VMEM_LIMIT),
    )(zt, held, v, yt, sy, sz)


def solution(mesh):
    in_specs = (P("col", "row", None), P("col", "row", None), P(), P(), P(), P(), P(), P())
    out_specs = P("col", "row", None)
    return jax.shard_map(body, mesh=mesh, in_specs=in_specs, out_specs=out_specs, check_vma=False)
```

```python
import functools

import jax
import jax.numpy as jnp
from jax import lax
from jax.experimental import pallas as pl
from jax.experimental.pallas import tpu as pltpu
from jax.sharding import PartitionSpec as P

WEIGHT = 0.5
STEP = 1000.0
MESH = pl.DeviceIdType.MESH
VMEM_LIMIT = 24 * 1024 * 1024


def shifted(a, by, fill):
    n = a.shape[1]
    lane = lax.broadcasted_iota(jnp.int32, a.shape, 1)
    if by > 0:
        return jnp.where(lane >= by, pltpu.roll(a, by, 1), fill)
    return jnp.where(lane < n + by, pltpu.roll(a, n + by, 1), fill)


def running_sum(a):
    by = 1
    while by < a.shape[1]:
        a = a + shifted(a, by, 0.0)
        by *= 2
    return a


def ladder(couple, sign):
    p00, p01, p10, p11 = 1.0 + couple, couple, jnp.ones_like(couple), couple
    by = 1
    while by < couple.shape[1]:
        q00, q01 = shifted(p00, sign * by, 1.0), shifted(p01, sign * by, 0.0)
        q10, q11 = shifted(p10, sign * by, 0.0), shifted(p11, sign * by, 1.0)
        n00, n01 = p00 * q00 + p01 * q10, p00 * q01 + p01 * q11
        n10, n11 = p10 * q00 + p11 * q10, p10 * q01 + p11 * q11
        scale = 1.0 / (n00 + n01 + n10 + n11)
        p00, p01, p10, p11 = n00 * scale, n01 * scale, n10 * scale, n11 * scale
        by *= 2
    return p00 / p10


def as_column(line, rows):
    n = line.shape[1]
    return jnp.transpose(jnp.broadcast_to(line, (n, n)))[:rows, :rows]


def block_of_inverse(diagonal, sums, n):
    i = lax.broadcasted_iota(jnp.int32, (n, n), 0)
    j = lax.broadcasted_iota(jnp.int32, (n, n), 1)
    near = jnp.where(i >= j, diagonal[:, :n], as_column(diagonal, n))
    return near * jnp.exp(-jnp.abs(as_column(sums, n) - sums[:, :n]))


def table_kernel(
    nr, nc, xf_ref, yf_ref, zf_ref, field_ref, xh_ref, xl_ref, xp_ref, ym_ref, yt_ref, zt_ref,
    held_ref, yhalo_ref, zhalo_ref, strips, edges, fetch_sem, strip_sem, send_sem, recv_sem,
):
    row, col = lax.axis_index("row"), lax.axis_index("col")
    zc, yc, _ = field_ref.shape
    tall = strips.shape[2]
    strip_copies = [
        pltpu.make_async_copy(
            field_ref.at[:, pl.ds(start, tall)], strips.at[side], strip_sem.at[side]
        )
        for side, start in ((0, yc - tall), (1, 0))
    ]
    for copy in strip_copies:
        copy.start()
    fetch = pltpu.make_async_copy(field_ref, held_ref, fetch_sem)
    fetch.start()
    places = [
        (row < nr - 1, row > 0, (row + 1, col)),
        (row > 0, row < nr - 1, (row - 1, col)),
        (col < nc - 1, col > 0, (row, col + 1)),
        (col > 0, col < nc - 1, (row, col - 1)),
    ]
    barrier = pltpu.get_barrier_semaphore()
    expected = 0
    for to, _, device in places:
        expected += to.astype(jnp.int32)

        @pl.when(to)
        def _():
            pl.semaphore_signal(barrier, inc=1, device_id=device, device_id_type=MESH)

    pl.semaphore_wait(barrier, expected)
    ends = [
        (edges.at[0], yhalo_ref.at[0]),
        (edges.at[1], yhalo_ref.at[1]),
        (field_ref.at[zc - 1], zhalo_ref.at[0]),
        (field_ref.at[0], zhalo_ref.at[1]),
    ]
    halo = [
        pltpu.make_async_remote_copy(
            src_ref=source, dst_ref=target, send_sem=send_sem.at[k], recv_sem=recv_sem.at[k],
            device_id=places[k][2], device_id_type=MESH,
        )
        for k, (source, target) in enumerate(ends)
    ]
    for k in (2, 3):
        @pl.when(places[k][0])
        def _():
            halo[k].start()

    for side in (0, 1):
        strip_copies[side].wait()
        for z in range(zc):
            at = tall - 1 if side == 0 else 0
            edges[side, z:z + 1] = strips[side, z, at:at + 1]

        @pl.when(places[side][0])
        def _():
            halo[side].start()

    for k in range(4):
        @pl.when(jnp.logical_not(places[k][1]))
        def _():
            target = ends[k][1]
            target[...] = jnp.zeros_like(target)

    given = [xf_ref[...], yf_ref[...], zf_ref[...]]
    length = -(-max(a.shape[1] for a in given) // 128) * 128
    lines = []
    for a in given:
        missing = length - a.shape[1]
        lines.append(jnp.concatenate([a, jnp.zeros((1, missing), a.dtype)], 1) if missing else a)
    faces = jnp.concatenate(lines + [jnp.zeros((5, length), jnp.float32)], axis=0)
    nb, bx = xh_ref.shape[0], xh_ref.shape[1]
    nx = nb * bx
    here = WEIGHT * STEP * faces
    above = shifted(here, -1, 0.0)
    e = ladder(here, 1)
    h = ladder(above, -1)
    pivot = above + e
    down = above / pivot
    inverse = 1.0 / pivot
    diag = 1.0 / (e + h - 1.0)
    ups = running_sum(jnp.log(jnp.maximum(here / (here + h), 1e-30)))
    downs = running_sum(jnp.log(jnp.maximum(down, 1e-30)))
    ups_before, downs_before = shifted(ups, 1, 0.0), shifted(downs, 1, 0.0)
    full, next_full = STEP * faces, STEP * shifted(faces, -1, 0.0)
    around = full + next_full

    xp_ref[2:3] = shifted(next_full, 1, 0.0)[0:1, :nx]
    xp_ref[3:4] = next_full[0:1, :nx]
    xp_ref[4:5] = around[0:1, :nx]
    for b in range(nb):
        first, last = b * bx, (b + 1) * bx - 1
        cols = slice(first, last + 1)
        high, low = split(block_of_inverse(diag[0:1, cols], ups[0:1, cols], bx))
        xh_ref[b] = high
        xl_ref[b] = low
        xp_ref[0:1, cols] = jnp.exp(ups[0:1, cols] - ups_before[0:1, first:first + 1])
        xp_ref[1:2, cols] = jnp.exp(downs[0:1, last:last + 1] - downs_before[0:1, cols])

    def own(values, which, start):
        shift = lax.rem(length - start, length)
        return pltpu.roll(values, shift, 1)[which:which + 1]

    def passes(which, start, count):
        u0, d0 = own(ups_before, which, start)[:, 0:1], own(downs_before, which, start)
        u1, d1 = own(ups, which, start), own(downs, which, start)[:, count - 1:count]
        return u1, u0, d1, jnp.exp(jnp.minimum(u1 - u0, 0.0)), jnp.exp(jnp.minimum(d1 - d0, 0.0))

    wide = -(-yc // 128) * 128
    y0 = row * yc
    sums, up_first, down_last, onward, backward = passes(1, y0, yc)
    block = block_of_inverse(own(diag, 1, y0)[:, :wide], sums[:, :wide], wide)[:yc, :yc]
    high = block.astype(jnp.bfloat16).astype(jnp.float32)
    ym_ref[:, 0:yc] = high
    ym_ref[:, yc:2 * yc] = high
    ym_ref[:, 2 * yc:3 * yc] = block - high
    lines = [onward, backward, own(full, 1, y0), own(next_full, 1, y0), own(around, 1, y0)]
    lines = [a[:, :wide] for a in lines] + [jnp.zeros((123, wide), jnp.float32)]
    yt_ref[...] = jnp.transpose(jnp.concatenate(lines, axis=0))[:yc]

    lane = lax.broadcasted_iota(jnp.int32, (1, 128), 1)
    low_weights = high_weights = jnp.zeros((1, 128), jnp.float32)
    for other in range(nr):
        last, first = (other + 1) * yc - 1, other * yc
        value = jnp.exp(jnp.minimum(up_first - ups[1:2, last:last + 1], 0.0))
        low_weights = jnp.where(lane == other, value, low_weights)
        value = jnp.exp(jnp.minimum(downs_before[1:2, first:first + 1] - down_last, 0.0))
        high_weights = jnp.where(lane == other, value, high_weights)

    z0 = col * zc
    _, _, _, onward, backward = passes(2, z0, zc)
    at = lax.broadcasted_iota(jnp.int32, (1, length), 1)
    over = jnp.where(at == zc - 1, own(diag, 2, z0), own(inverse, 2, z0))
    into = jnp.where(at == 0, 0.0, own(here, 2, z0) * over)
    lines = [
        over, into, own(down, 2, z0), own(full, 2, z0), own(next_full, 2, z0), onward, backward,
    ]
    for k, line in enumerate(lines):
        zt_ref[k:k + 1] = line[:, :128]
    zt_ref[7:8] = low_weights
    zt_ref[8:9] = high_weights
    zt_ref[9:10] = own(around, 2, z0)[:, :128]
    zt_ref[10:16] = jnp.zeros((6, 128), jnp.float32)
    for k in range(4):
        @pl.when(places[k][0])
        def _():
            halo[k].wait_send()

        @pl.when(places[k][1])
        def _():
            halo[k].wait_recv()

    fetch.wait()


def on_chip(*shape):
    return pltpu.VMEM(shape, jnp.float32)


def split(a):
    high = a.astype(jnp.bfloat16)
    return high, (a - high.astype(jnp.float32)).astype(jnp.bfloat16)


def dot(a, b):
    return jnp.dot(a, b, preferred_element_type=jnp.float32)


def sweep_kernel(
    planes, zt_ref, u_ref, yhalo_ref, zhalo_ref,
    rea_ref, yt_ref, xh_ref, xl_ref, xp_ref, ym_ref, v_ref, ye_ref, ze_ref,
):
    step, steps = pl.program_id(0), pl.num_programs(0)
    zc, yc, nx = u_ref.shape
    nb, bx = xh_ref.shape[0], xh_ref.shape[1]
    kx, kxn = xp_ref[2:3], xp_ref[3:4]
    ky, kyn = yt_ref[:, 2:3], yt_ref[:, 3:4]
    sub = lax.broadcasted_iota(jnp.int32, (yc, nx), 0)

    @pl.when(step == 0)
    def _():
        v_ref[0] = jnp.zeros((yc, nx), jnp.float32)

    below = jnp.where(step == 0, zhalo_ref[0], u_ref[jnp.maximum(step * planes - 1, 0)])
    above_last = u_ref[jnp.minimum((step + 1) * planes, zc - 1)]
    above_last = jnp.where(step == steps - 1, zhalo_ref[1], above_last)
    changes = []
    for p in range(planes):
        z = step * planes + p
        u = u_ref[z]
        above = u_ref[z + 1] if p + 1 < planes else above_last
        down = jnp.where(sub == 0, yhalo_ref[0, pl.ds(z, 1)], pltpu.roll(u, 1, 0))
        upper = jnp.where(sub == yc - 1, yhalo_ref[1, pl.ds(z, 1)], pltpu.roll(u, yc - 1, 0))
        total = kxn * pltpu.roll(u, nx - 1, 1) + kx * pltpu.roll(u, 1, 1)
        total += kyn * upper + ky * down
        total += zt_ref[4, z] * above + zt_ref[3, z] * below
        centre = STEP * rea_ref[p] * (1.0 - u * u) - (xp_ref[4:5] + (yt_ref[:, 4:5] + zt_ref[9, z]))
        changes.append(total + u * centre)
        below = u
    change = jnp.concatenate(changes, axis=0) if planes > 1 else changes[0]
    local = []
    for b in range(nb):
        high, low = split(change[:, b * bx:(b + 1) * bx])
        local.append(dot(high, xh_ref[b]) + (dot(high, xl_ref[b]) + dot(low, xh_ref[b])))
    rows = planes * yc
    from_left = [jnp.zeros((rows, 1), jnp.float32)]
    from_right = [jnp.zeros((rows, 1), jnp.float32)]
    for b in range(nb - 1):
        through = xp_ref[0:1, (b + 1) * bx - 1:(b + 1) * bx]
        from_left.append(from_left[-1] * through + local[b][:, bx - 1:bx])
        c = nb - 1 - b
        through = xp_ref[1:2, c * bx:c * bx + 1]
        from_right.append(from_right[-1] * through + local[c][:, 0:1])
    from_right.reverse()
    solved = jnp.concatenate(
        [
            local[b]
            + xp_ref[0:1, b * bx:(b + 1) * bx] * from_left[b]
            + xp_ref[1:2, b * bx:(b + 1) * bx] * from_right[b]
            for b in range(nb)
        ],
        axis=1,
    )
    carry = v_ref[jnp.maximum(step * planes - 1, 0)]
    for p in range(planes):
        z = step * planes + p
        high, low = split(solved[p * yc:(p + 1) * yc])
        w = dot(ym_ref[...].astype(jnp.bfloat16), jnp.concatenate([high, low, high], axis=0))
        carry = zt_ref[0, z] * w + zt_ref[1, z] * carry
        v_ref[z] = carry

    @pl.when(step == steps - 1)
    def _():
        wide = 256 if nx % 256 == 0 else nx
        for x in range(nx // wide):
            cols = slice(x * wide, (x + 1) * wide)
            top = v_ref[zc - 1, :, cols]
            ze_ref[1, :, cols] = top
            ye_ref[0, zc - 1:zc, cols] = top[0:1]
            ye_ref[1, zc - 1:zc, cols] = top[yc - 1:yc]

            def back(i, value):
                z = zc - 2 - i
                value = v_ref[z, :, cols] + zt_ref[2, z] * value
                v_ref[z, :, cols] = value
                ye_ref[0, pl.ds(z, 1), cols] = value[0:1]
                ye_ref[1, pl.ds(z, 1), cols] = value[yc - 1:yc]
                return value

            ze_ref[0, :, cols] = lax.fori_loop(0, zc - 1, back, top)


def exchange_kernel(
    nr, nc, chunks, zt_ref, yp_ref, ye_ref, ze_ref, sy_ref, sz_ref,
    ybuf, zbuf, zsend, esend, ebuf, ysend_sem, yrecv_sem, zsend_sem, zrecv_sem,
    esend_sem, erecv_sem,
):
    row, col = lax.axis_index("row"), lax.axis_index("col")
    zc, nx = ye_ref.shape[1], ye_ref.shape[2]
    yc = ze_ref.shape[1]
    has_low, has_high = col > 0, col < nc - 1
    barrier = pltpu.get_barrier_semaphore()
    for other in range(nr):
        @pl.when(other != row)
        def _():
            pl.semaphore_signal(barrier, inc=1, device_id=(other, col), device_id_type=MESH)

    @pl.when(has_low)
    def _():
        pl.semaphore_signal(barrier, inc=1, device_id=(row, col - 1), device_id_type=MESH)

    @pl.when(has_high)
    def _():
        pl.semaphore_signal(barrier, inc=1, device_id=(row, col + 1), device_id_type=MESH)

    pl.semaphore_wait(barrier, nr - 1 + has_low.astype(jnp.int32) + has_high.astype(jnp.int32))

    def y_copy(side, other, slot):
        return pltpu.make_async_remote_copy(
            src_ref=ye_ref.at[1 - side],
            dst_ref=ybuf.at[side, slot],
            send_sem=ysend_sem.at[side, other],
            recv_sem=yrecv_sem.at[side, slot],
            device_id=(other, col),
            device_id_type=MESH,
        )

    for other in range(nr):
        @pl.when(other > row)
        def _():
            y_copy(0, other, row).start()

        @pl.when(other < row)
        def _():
            y_copy(1, other, row).start()

    part = yc // chunks

    def z_copy(side, k):
        rows = pl.ds(k * part, part)
        return pltpu.make_async_remote_copy(
            src_ref=zsend.at[side, rows],
            dst_ref=zbuf.at[side, rows],
            send_sem=zsend_sem.at[side, k],
            recv_sem=zrecv_sem.at[side, k],
            device_id=(row, col + (1 - 2 * side)),
            device_id_type=MESH,
        )

    def scan(side):
        source, target = (has_low, has_high) if side == 0 else (has_high, has_low)
        edge, z = (1, zc - 1) if side == 0 else (0, 0)
        through = zt_ref[5 + side, z]
        for k in range(chunks):
            rows = slice(k * part, (k + 1) * part)

            @pl.when(source)
            def _():
                z_copy(side, k).wait_recv()
                sz_ref[side, rows] = zbuf[side, rows]

            @pl.when(jnp.logical_not(source))
            def _():
                sz_ref[side, rows] = jnp.zeros((part, nx), jnp.float32)

            @pl.when(target)
            def _():
                zsend[side, rows] = ze_ref[edge, rows] + through * sz_ref[side, rows]
                z_copy(side, k).start()

    low_half = col < nc // 2

    @pl.when(low_half)
    def _():
        scan(0)

    scan(1)

    @pl.when(jnp.logical_not(low_half))
    def _():
        scan(0)

    for k in range(2):
        esend[0, k:k + 1] = sz_ref[k, yc - 1:yc]
        esend[1, k:k + 1] = sz_ref[k, 0:1]

    def e_copy(side, other, slot):
        return pltpu.make_async_remote_copy(
            src_ref=esend.at[side],
            dst_ref=ebuf.at[side, slot],
            send_sem=esend_sem.at[side, other],
            recv_sem=erecv_sem.at[side, slot],
            device_id=(other, col),
            device_id_type=MESH,
        )

    for other in range(nr):
        @pl.when(other > row)
        def _():
            e_copy(0, other, row).start()

        @pl.when(other < row)
        def _():
            e_copy(1, other, row).start()

    sy_ref[...] = jnp.zeros_like(sy_ref)
    for other in range(nr):
        @pl.when(other < row)
        def _():
            y_copy(0, other, other).wait_recv()
            sy_ref[0] += zt_ref[7, other] * ybuf[0, other]

        @pl.when(other > row)
        def _():
            y_copy(1, other, other).wait_recv()
            sy_ref[1] += zt_ref[8, other] * ybuf[1, other]

    for other in range(nr):
        for side, here in ((0, other < row), (1, other > row)):
            @pl.when(here)
            def _():
                e_copy(side, other, other).wait_recv()
                coefficients = zt_ref[7 + side, other] * yp_ref[:, side:side + 1]
                for k in range(2):
                    sz_ref[k] += coefficients * ebuf[side, other, k:k + 1]

    for k in range(chunks):
        @pl.when(has_high)
        def _():
            z_copy(0, k).wait_send()

        @pl.when(has_low)
        def _():
            z_copy(1, k).wait_send()

    for other in range(nr):
        for side, there in ((0, other > row), (1, other < row)):
            @pl.when(there)
            def _():
                y_copy(side, other, row).wait_send()
                e_copy(side, other, row).wait_send()


def finish_kernel(planes, zt_ref, u_ref, v_ref, yp_ref, sy_ref, sz_ref, out_ref):
    yb, ya = yp_ref[:, 0:1], yp_ref[:, 1:2]
    for p in range(planes):
        z = pl.program_id(0) * planes + p
        value = u_ref[z] + v_ref[z]
        value += yb * sy_ref[0, pl.ds(z, 1)] + ya * sy_ref[1, pl.ds(z, 1)]
        out_ref[p] = value + zt_ref[5, z] * sz_ref[0] + zt_ref[6, z] * sz_ref[1]


def body(u, reaction, x_faces, y_faces, z_faces, x_inverse, y_inverse, z_inverse):
    zc, yc, nx = u.shape
    nr, nc = lax.axis_size("row"), lax.axis_size("col")
    f32 = jnp.float32

    tall = 8 if yc % 8 == 0 else yc
    bx = 256 if nx % 256 == 0 else nx
    nb = nx // bx
    smem = pl.BlockSpec(memory_space=pltpu.SMEM)
    vmem = pl.BlockSpec(memory_space=pltpu.VMEM)
    xh, xl, xp, ym, yt, zt, held, yhalo, zhalo = pl.pallas_call(
        functools.partial(table_kernel, nr, nc),
        in_specs=[vmem, vmem, vmem, pl.BlockSpec(memory_space=pltpu.HBM)],
        out_specs=[vmem] * 9,
        out_shape=[
            jax.ShapeDtypeStruct((nb, bx, bx), jnp.bfloat16),
            jax.ShapeDtypeStruct((nb, bx, bx), jnp.bfloat16),
            jax.ShapeDtypeStruct((8, nx), f32),
            jax.ShapeDtypeStruct((yc, 3 * yc), f32),
            jax.ShapeDtypeStruct((yc, 128), f32),
            jax.ShapeDtypeStruct((16, 128), f32),
            on_chip(zc, yc, nx),
            on_chip(2, zc, nx),
            on_chip(2, yc, nx),
        ],
        scratch_shapes=[
            pltpu.VMEM((2, zc, tall, nx), f32),
            pltpu.VMEM((2, zc, nx), f32),
            pltpu.SemaphoreType.DMA(()),
            pltpu.SemaphoreType.DMA((2,)),
            pltpu.SemaphoreType.DMA((4,)),
            pltpu.SemaphoreType.DMA((4,)),
        ],
        compiler_params=pltpu.CompilerParams(
            collective_id=1, has_side_effects=True, vmem_limit_bytes=VMEM_LIMIT
        ),
        cost_estimate=pl.CostEstimate(flops=40000000, bytes_accessed=1 << 20, transcendentals=0),
    )(x_faces[None], y_faces[None], z_faces[None], pltpu.with_memory_space_constraint(u, pltpu.HBM))

    planes = next(p for p in (8, 4, 2, 1) if zc % p == 0)
    last = next(p for p in (8, 4, 2, 1) if zc % p == 0)
    reaction = pltpu.with_memory_space_constraint(reaction, pltpu.HBM)

    slab = pl.BlockSpec((planes, yc, nx), lambda step: (step, 0, 0))
    v, ye, ze = pl.pallas_call(
        functools.partial(sweep_kernel, planes),
        grid=(zc // planes,),
        in_specs=[
            smem, vmem, vmem, vmem, slab,
            vmem, vmem, vmem, vmem, vmem,
        ],
        out_specs=[vmem, vmem, vmem],
        out_shape=[
            on_chip(zc, yc, nx),
            jax.ShapeDtypeStruct((2, zc, nx), f32),
            jax.ShapeDtypeStruct((2, yc, nx), f32),
        ],
        compiler_params=pltpu.CompilerParams(vmem_limit_bytes=VMEM_LIMIT),
    )(zt, held, yhalo, zhalo, reaction, yt, xh, xl, xp, ym)

    chunks = yc // 8 if yc % 8 == 0 else 1
    sy, sz = pl.pallas_call(
        functools.partial(exchange_kernel, nr, nc, chunks),
        in_specs=[smem, vmem, vmem, vmem],
        out_specs=[vmem, vmem],
        out_shape=[
            jax.ShapeDtypeStruct((2, zc, nx), f32),
            jax.ShapeDtypeStruct((2, yc, nx), f32),
        ],
        scratch_shapes=[
            pltpu.VMEM((2, nr, zc, nx), f32),
            pltpu.VMEM((2, yc, nx), f32),
            pltpu.VMEM((2, yc, nx), f32),
            pltpu.VMEM((2, 2, nx), f32),
            pltpu.VMEM((2, nr, 2, nx), f32),
            pltpu.SemaphoreType.DMA((2, nr)),
            pltpu.SemaphoreType.DMA((2, nr)),
            pltpu.SemaphoreType.DMA((2, chunks)),
            pltpu.SemaphoreType.DMA((2, chunks)),
            pltpu.SemaphoreType.DMA((2, nr)),
            pltpu.SemaphoreType.DMA((2, nr)),
        ],
        compiler_params=pltpu.CompilerParams(
            collective_id=0, has_side_effects=True, vmem_limit_bytes=VMEM_LIMIT
        ),
    )(zt, yt, ye, ze)

    return pl.pallas_call(
        functools.partial(finish_kernel, last),
        grid=(zc // last,),
        in_specs=[smem, vmem, vmem, vmem, vmem, vmem],
        out_specs=pl.BlockSpec((last, yc, nx), lambda step: (step, 0, 0)),
        out_shape=jax.ShapeDtypeStruct((zc, yc, nx), f32),
        compiler_params=pltpu.CompilerParams(vmem_limit_bytes=VMEM_LIMIT),
    )(zt, held, v, yt, sy, sz)


def solution(mesh):
    in_specs = (P("col", "row", None), P("col", "row", None), P(), P(), P(), P(), P(), P())
    out_specs = P("col", "row", None)
    return jax.shard_map(body, mesh=mesh, in_specs=in_specs, out_specs=out_specs, check_vma=False)
```
